32 devices in a mesh: member: 8 (over z, x), cell: 4 (over y, core).
Axes of the slice: x: 2, y: 2, z: 4, core: 2. Of those that a mesh axis runs over, the one named last changes fastest.
Arguments:
- latent: bfloat16 [8, 6144, 1024], P('member', 'cell'), may hold values from -6 to 6
- w_in: bfloat16 [1024, 1024], replicated, may hold values from -0.1875 to 0.1875
- w_out: bfloat16 [1024, 96], replicated, may hold values from -0.1875 to 0.1875
- target: bfloat16 [96, 6144], P(None, 'cell'), may hold values from -6 to 6
- cell_mask: int32 [6144], P('cell'), may hold values 0 or 1
Outputs:
- grad_w_in: float32 [1024, 1024], P(('member', 'cell'))
- grad_w_out: float32 [1024, 96], P(('member', 'cell'))
The draws below stay inside these ranges and needn't reach their ends.
All inputs are finite; a program needn't handle non-finite values. No bound on the sum of `cell_mask` on one device may be relied on, other than what follows from the above.
Results may differ from the reference program's by a relative error of at most 0.0055.
Values may be sent and summed in bfloat16 or wider, within the bound.
A program may use at most 64 MiB of HBM per device.

```python
import jax
import jax.numpy as jnp
from jax import lax

LATENT = 1024
HIDDEN_SIZE = 1024
FIELDS = 96
CELLS = 6144
MEMBERS = 8


def plant(values, stream_key, low, top_value):
    longest = values.shape.index(max(values.shape))
    spots = []
    for shift in (0, 1):
        where = [jax.random.randint(jax.random.fold_in(stream_key, axis), (), 0, length) for axis, length in enumerate(values.shape)]
        where[longest] = (where[longest] + shift) % values.shape[longest]
        spots.append(tuple(where))
    return values.at[spots[0]].set(low).at[spots[1]].set(top_value)


def with_spikes(array, key, source, target, parts, factor):
    owner, partner = [(jnp.arange(array.shape[axis_at]) // (array.shape[axis_at] // parts)).reshape([-1 if axis == axis_at else 1 for axis in range(array.ndim)]) for axis_at in (source, target)]
    chosen = jax.random.permutation(key, parts)[partner]
    strong = (owner == chosen) | (owner == (partner + parts // 2) % parts)
    return jnp.where(strong, factor * array, array)


def levels(key, shape, shards, least, largest):
    def one(dim, shards_of):
        steps = jax.random.uniform(jax.random.fold_in(jax.random.fold_in(key, 6), dim), (shards_of,), jnp.float32, least / len(shards), largest / len(shards))
        return jnp.repeat(jnp.exp(steps), shape[dim] // shards_of).reshape((-1,) + (1,) * (len(shape) - dim - 1))

    factor_of = one(*shards[0])
    for cut in shards[1:]:
        factor_of = factor_of * one(*cut)
    return factor_of


def centred(key, extent, spread, reach, pieces=(), held_as=jnp.bfloat16):
    level = levels(key, extent, pieces, -0.22, 0.18) if pieces else 1.0
    result = jax.random.normal(key, extent, jnp.float32) * spread * level
    return jnp.minimum(jnp.maximum(result, -reach), reach).astype(held_as)


def heavy_noise(own_key, shape, deviation, most, cuts, heavy, dtype=jnp.bfloat16):
    values = deviation * jax.random.normal(own_key, shape, jnp.float32)
    if cuts:
        values = values * levels(own_key, shape, cuts, -0.22, 0.18)
    return jnp.clip(with_spikes(values, jax.random.fold_in(own_key, 3), *heavy), -most, most).astype(dtype)


def setup_inputs(seed: int = 0) -> dict:
    key_of = jax.random.split(jax.random.key(seed), 6)
    latent = heavy_noise(key_of[0], (MEMBERS, CELLS, LATENT), 1.0, 6.0, ((0, 8), (1, 4)), (1, 2, 4, 2.0))
    w_in = centred(key_of[1], (LATENT, HIDDEN_SIZE), LATENT ** -0.5, 0.1875)
    w_out = centred(key_of[2], (HIDDEN_SIZE, FIELDS), HIDDEN_SIZE ** -0.5, 0.1875)
    target = centred(key_of[3], (FIELDS, CELLS), 1.0, 6.0, ((1, 4),))
    cell_mask = plant((jax.random.randint(key_of[4], (CELLS,), 0, 4) < 3).astype(jnp.int32), jax.random.fold_in(key_of[4], 1), 0, 1)
    return dict(latent=latent, w_in=w_in, w_out=w_out, target=target, cell_mask=cell_mask)


def kernel_fn(diff):
    return diff / jnp.sqrt(1.0 + diff * diff)

def silu_slope(pre):
    gate = jax.nn.sigmoid(pre)
    return gate * (1.0 + pre * (1.0 - gate))

def decode(member_latent, w_in, w_out):
    pre = jnp.dot(member_latent, w_in, preferred_element_type=jnp.float32)
    hidden = jax.nn.silu(pre).astype(jnp.bfloat16)
    fields = lax.dot_general(w_out, hidden, (((0,), (1,)), ((), ())), preferred_element_type=jnp.float32).astype(jnp.bfloat16)
    return (pre, hidden, fields)

def reference(latent, w_in, w_out, target, cell_mask):
    members = latent.shape[0]
    cells = latent.shape[1]
    scale = 1.0 / jnp.sqrt(jnp.float32(cells))
    fields = lax.map(lambda one: decode(one, w_in, w_out)[2], latent)
    wide = fields.astype(jnp.float32)
    pair = lax.map(lambda own: lax.optimization_barrier(jnp.sum(kernel_fn(own[None] - wide), axis=0)), wide)
    weight = cell_mask.astype(jnp.float32) * scale / members
    own_term = kernel_fn(wide - target.astype(jnp.float32)[None])
    grad_fields = (weight[None, None] * (own_term - pair / members)).astype(jnp.bfloat16)

    def accumulate(carry, item):
        member_latent, member_grad = item
        pre, hidden, unused = decode(member_latent, w_in, w_out)
        back = lax.dot_general(member_grad, w_out, (((0,), (1,)), ((), ())), preferred_element_type=jnp.float32)
        grad_pre = (back * silu_slope(pre)).astype(jnp.bfloat16)
        grad_in = lax.dot_general(member_latent, grad_pre, (((0,), (0,)), ((), ())), preferred_element_type=jnp.float32)
        grad_out = lax.dot_general(hidden, member_grad, (((0,), (1,)), ((), ())), preferred_element_type=jnp.float32)
        return ((carry[0] + grad_in, carry[1] + grad_out), None)
    start = (jnp.zeros(w_in.shape, jnp.float32), jnp.zeros(w_out.shape, jnp.float32))
    totals, unused = lax.scan(accumulate, start, (latent, grad_fields))
    return (totals[0], totals[1])
```

```python
import functools
import math

import jax
import jax.numpy as jnp
from jax import lax
from jax.experimental import pallas as pl
from jax.experimental.pallas import tpu as pltpu
from jax.sharding import PartitionSpec as P

MESH = pl.DeviceIdType.MESH
BF = jnp.bfloat16
F32 = jnp.float32
LANES = 128
PHASES = 3


def sigmoid(v):
    return 0.5 * jnp.tanh(0.5 * v) + 0.5


def smooth(d):
    return d * lax.rsqrt(1.0 + d * d)


def mm(a, b):
    return jnp.dot(a, b, preferred_element_type=F32)


def pack(f, width):
    spare = LANES - width
    n = width // spare
    q = f.shape[0] // (n + 1)
    lane = lax.broadcasted_iota(jnp.int32, (q, LANES), 1)
    last = f[n * q :]
    parts = []
    for k in range(n):
        parts.append(jnp.where(lane < width, f[k * q : (k + 1) * q], pltpu.roll(last, width - spare * k, 1)))
    return jnp.concatenate(parts, axis=0)


def unpack_last(p, width):
    spare = LANES - width
    n = width // spare
    q = p.shape[0] // n
    lane = lax.broadcasted_iota(jnp.int32, (q, LANES), 1)
    out = pltpu.roll(p[:q], spare, 1)
    for k in range(1, n):
        out = jnp.where(lane < spare * k, out, pltpu.roll(p[k * q : (k + 1) * q], spare * (k + 1), 1))
    return out


def body(
    M, CN, WA,
    lat_hbm, w_in_hbm, w_out_hbm, target_hbm, mask_hbm, out,
    lat, w_in, wo, target, mask, slope, hid, gp, gfu, lat_t, hid_t, tgt_t, wgt_t,
    fsend, frecv, gsend, gf,
    acc, acc_f, acc_b, r1, k2, a2, b2, ra, rb, k3, a3, b3, r3a, r3b, sz, rz,
    sem_in, sem_fs, sem_fr, sem_gs, sem_gr,
    sem1s, sem1r, sem2as, sem2ar, sem2bs, sem2br, sem3as, sem3ar, sem3bs, sem3br, sem4s, sem4r,
):
    me = lax.axis_index("member")
    cell = lax.axis_index("cell")
    core = lax.rem(cell, 2)
    grp = cell // 2
    G = CN // 2
    HM = M // 2
    PB = M // 2
    z = me // 2
    x = lax.rem(me, 2)
    half = me // HM
    PH = fsend.shape[0]
    CH, D = lat.shape[2:]
    H = w_in.shape[1]
    FD = w_out_hbm.shape[0]
    B = HM * CH
    K = M * CH
    C = PH * CH
    N = PH * K
    PR = fsend.shape[2]
    W = acc.shape[2]
    r = D // (M * CN)
    scale = 1.0 / (float(N * CN) ** 0.5) / M
    pair_core = (me, grp * 2 + 1 - core)
    pair_x = (me + 1 - 2 * x, cell)

    barrier = pltpu.get_barrier_semaphore()
    for d in range(1, M):
        pl.semaphore_signal(barrier, inc=1, device_id=(lax.rem(me + d, M), cell), device_id_type=MESH)
    pl.semaphore_signal(barrier, inc=1, device_id=pair_core, device_id_type=MESH)
    for d in range(1, G):
        pl.semaphore_signal(
            barrier, inc=1, device_id=(me, lax.rem(grp + d, G) * 2 + core), device_id_type=MESH
        )

    def which_half(i):
        return (1 - half) * (1 - lax.rem(i, 2)) + half * lax.rem(i, 2)

    def load(i):
        h = i // 2
        hf = which_half(i)
        return pltpu.make_async_copy(
            lat_hbm.at[pl.ds(hf * HM, HM), pl.ds(pl.multiple_of(h * CH, CH), CH), :],
            lat.at[2 * h + hf],
            sem_in.at[i],
        )

    load_w = pltpu.make_async_copy(w_in_hbm, w_in, sem_in.at[2 * PH])
    load_o = pltpu.make_async_copy(w_out_hbm, wo.at[pl.ds(0, FD), :], sem_in.at[2 * PH + 1])
    load_t = pltpu.make_async_copy(target_hbm, target, sem_in.at[2 * PH + 2])
    load_m = pltpu.make_async_copy(mask_hbm, mask, sem_in.at[2 * PH + 3])
    load_w.start()
    load(0).start()
    load_o.start()
    for i in range(1, 2 * PH):
        load(i).start()
    load_t.start()
    load_m.start()
    wo[FD:, :] = jnp.zeros((LANES - FD, H), BF)

    def f_copy(h, t):
        return pltpu.make_async_remote_copy(
            fsend.at[h, t], frecv.at[h, me], sem_fs.at[h, t], sem_fr.at[h, me],
            device_id=(t, cell), device_id_type=MESH,
        )

    def f_wait(h, j):
        pltpu.make_async_remote_copy(
            fsend.at[h, j], frecv.at[h, j], sem_fs.at[h, j], sem_fr.at[h, j],
            device_id=(j, cell), device_id_type=MESH,
        ).wait_recv()

    def g_copy(h, t):
        return pltpu.make_async_remote_copy(
            gsend.at[h, t], gf.at[h, me], sem_gs.at[h, t], sem_gr.at[h, me],
            device_id=(t, cell), device_id_type=MESH,
        )

    def g_wait(h, j):
        pltpu.make_async_remote_copy(
            gsend.at[h, j], gf.at[h, j], sem_gs.at[h, j], sem_gr.at[h, j],
            device_id=(j, cell), device_id_type=MESH,
        ).wait_recv()

    def other_half(k):
        return (1 - half) * HM + lax.rem(me + k, HM)

    def same_half(k):
        return half * HM + lax.rem(me + k, HM)

    def c1(i):
        return pltpu.make_async_remote_copy(
            acc_b.at[i, 1 - core], r1.at[i], sem1s.at[i], sem1r.at[i],
            device_id=pair_core, device_id_type=MESH,
        )

    def c2a(i, d):
        g = lax.rem(grp + d, G)
        return pltpu.make_async_remote_copy(
            a2.at[i, g], ra.at[i, d - 1], sem2as.at[i, d - 1], sem2ar.at[i, d - 1],
            device_id=(me, g * 2 + core), device_id_type=MESH,
        )

    def c2b(i):
        return pltpu.make_async_remote_copy(
            b2.at[i, 1 - x], rb.at[i], sem2bs.at[i], sem2br.at[i],
            device_id=pair_x, device_id_type=MESH,
        )

    def c3a(i):
        return pltpu.make_async_remote_copy(
            a3.at[i], r3a.at[i], sem3as.at[i], sem3ar.at[i],
            device_id=pair_x, device_id_type=MESH,
        )

    def c3b(i, d):
        g = lax.rem(grp + d, G)
        return pltpu.make_async_remote_copy(
            b3.at[i, g], r3b.at[i, d - 1], sem3bs.at[i, d - 1], sem3br.at[i, d - 1],
            device_id=(me, g * 2 + core), device_id_type=MESH,
        )

    def block_of(i):
        return lax.rem(z + 1 + i, PB)

    def c4(i):
        return pltpu.make_async_remote_copy(
            sz.at[i], rz.at[i], sem4s.at[i], sem4r.at[i],
            device_id=(block_of(i) * 2 + x, cell), device_id_type=MESH,
        )

    def forward(i, carry):
        h = i // 2
        hf = which_half(i)
        blk = 2 * h + hf
        rows = pl.ds(pl.multiple_of(blk * B, B), B)
        load(i).wait()
        v = mm(lat[blk].reshape(B, D), w_in[...])
        s = sigmoid(v)
        slope[rows, :] = s * (1.0 + v * (1.0 - s))
        hb = (v * s).astype(BF)
        hid[rows, :] = hb
        f = lax.dot_general(hb, wo[...], (((1,), (1,)), ((), ())), preferred_element_type=F32)

        @pl.when(i == 0)
        def _():
            pl.semaphore_wait(barrier, M - 1 + 1 + G - 1)

        for k in range(HM):
            t = hf * HM + k
            p = pack(f[k * CH : (k + 1) * CH], FD).astype(BF)
            fsend[h, t] = p

            @pl.when(t == me)
            def _():
                frecv[h, me] = p

            @pl.when(t != me)
            def _():
                f_copy(h, t).start()

        return carry

    with jax.named_scope("loadw"):
        load_w.wait()
        load_o.wait()
    with jax.named_scope("forward"):
        lax.fori_loop(0, 2 * PH, forward, 0)

    with jax.named_scope("prep"):
        load_t.wait()
        load_m.wait()
        NB = tgt_t.shape[0] // LANES
        b0 = jnp.minimum(me * C // LANES, N // LANES - NB)
        for b in range(NB):
            cols = pl.ds(pl.multiple_of((b0 + b) * LANES, LANES), LANES)
            tgt_t[b * LANES : (b + 1) * LANES, :FD] = target[:, cols].astype(F32).T
        for b in range(N // LANES):
            cols = slice(LANES * b, LANES * b + LANES)
            w = mask[cols].astype(F32) * scale
            wgt_t[cols, :] = jnp.broadcast_to(w[None, :], (8, LANES)).T
        for h in range(PH):
            for b in range(K // LANES):
                lat_t[h, :, LANES * b : LANES * b + LANES] = (
                    lat[2 * h : 2 * h + 2].reshape(K, D)[LANES * b : LANES * b + LANES, :].T
                )

    RB = 16 if PR % 16 == 0 else PR

    def phase(h, carry):
        for k in range(1, HM):
            f_wait(h, same_half(k))
        for k in range(HM):
            f_wait(h, other_half(k))
        own = pl.multiple_of(me * C - b0 * LANES + h * CH, 8)
        tp = pack(tgt_t[pl.ds(own, CH), :], FD)
        wp = pack(
            jnp.broadcast_to(wgt_t[pl.ds(pl.multiple_of(me * C + h * CH, 8), CH), 0:1], (CH, LANES)), FD
        )
        for b in range(PR // RB):
            rows = slice(b * RB, (b + 1) * RB)
            vals = [frecv[h, j, rows, :].astype(F32) for j in range(M)]
            total = [None] * M
            for a in range(M):
                for c in range(a + 1, M):
                    k = smooth(vals[a] - vals[c])
                    total[a] = k if total[a] is None else total[a] + k
                    total[c] = -k if total[c] is None else total[c] - k
            for a in range(M):
                g = wp[rows] * (smooth(vals[a] - tp[rows]) - total[a] * (1.0 / M))
                gsend[h, a, rows, :] = g.astype(BF)
        for k in range(HM):
            g_copy(h, other_half(k)).start()
        for k in range(1, HM):
            g_copy(h, same_half(k)).start()
        gf[h, me] = gsend[h, me]
        return carry

    with jax.named_scope("pairs"):
        lax.fori_loop(0, PH, phase, 0)

    with jax.named_scope("hidt"):
        for h in range(PH):
            for b in range(K // LANES):
                at = h * K + LANES * b
                hid_t[h, :, LANES * b : LANES * b + LANES] = hid[at : at + LANES, :].T

    def back(h, hf):
        blk = 2 * h + hf
        for k in range(HM):
            p = gf[h, hf * HM + k]
            at = pl.multiple_of(blk * B + k * CH, CH)
            gfu[pl.ds(at, PR), :] = p
            gfu[pl.ds(pl.multiple_of(at + PR, CH - PR), CH - PR), :] = unpack_last(p.astype(F32), FD).astype(BF)
        rows = pl.ds(pl.multiple_of(blk * B, B), B)
        gp[rows, :] = (mm(gfu[rows, :], wo[...]) * slope[rows, :]).astype(BF)

    def gather(h):
        for k in range(1, HM):
            g_wait(h, same_half(k))
        back(h, half)
        for k in range(HM):
            g_wait(h, other_half(k))
        back(h, 1 - half)

    def terms(h, p):
        rows = pl.ds(pl.multiple_of(p * (2 * r * CN), 2 * r * CN), 2 * r * CN)
        at = pl.ds(pl.multiple_of(h * K, K), K)
        return mm(lat_t[h, rows, :], gp[at, :]), mm(hid_t[h, rows, :], gfu[at, :])

    def early(h, carry):
        gather(h)

        def add(p, c):
            a, b = terms(h, p)

            @pl.when(h == 0)
            def _():
                acc[p, :, :H] = a
                acc[p, :, H:] = b

            @pl.when(h > 0)
            def _():
                acc[p, :, :H] += a
                acc[p, :, H:] += b

            return c

        return lax.fori_loop(0, PB, add, carry)

    with jax.named_scope("early"):
        lax.fori_loop(0, PH - 1, early, 0)

    with jax.named_scope("gather"):
        gather(PH - 1)

    def first(i, carry):
        p = block_of(i)
        a, b = terms(PH - 1, p)
        a = a + acc[p, :, :H]
        b = b + acc[p, :, H:]
        for s in range(2):
            for c in range(CN):
                at = (s * CN + c) * r
                u, v = a[at : at + r], b[at : at + r]
                acc_f[i, c % 2, s, c // 2, :, :H] = u
                acc_f[i, c % 2, s, c // 2, :, H:] = v
                acc_b[i, c % 2, s, c // 2, :, :H] = u.astype(BF)
                acc_b[i, c % 2, s, c // 2, :, H:] = v.astype(BF)
        c1(i).start()
        return carry

    with jax.named_scope("first"):
        lax.fori_loop(0, PB, first, 0)

    def second(i, carry):
        c1(i).wait_recv()
        for s in range(2):
            for g in range(G):
                v = acc_f[i, core, s, g] + r1[i, s, g].astype(F32)
                k2[i, s, g] = v
                a2[i, g, s] = v[:, :WA].astype(BF)
                b2[i, s, g] = v[:, WA:].astype(BF)
        for d in range(1, G):
            c2a(i, d).start()
        c2b(i).start()
        return carry

    with jax.named_scope("second"):
        lax.fori_loop(0, PB, second, 0)

    def third(i, carry):
        for d in range(1, G):
            c2a(i, d).wait_recv()
        away = k2[i, 1 - x, grp, :, :WA]
        keep = k2[i, x, grp, :, :WA]
        for d in range(1, G):
            away = away + ra[i, d - 1, 1 - x].astype(F32)
            keep = keep + ra[i, d - 1, x].astype(F32)
        a3[i] = away.astype(BF)
        c3a(i).start()
        k3[i, :, :WA] = keep
        c2b(i).wait_recv()
        for g in range(G):
            b3[i, g] = (k2[i, x, g, :, WA:] + rb[i, g].astype(F32)).astype(BF)
        for d in range(1, G):
            c3b(i, d).start()
        k3[i, :, WA:] = k2[i, x, grp, :, WA:] + rb[i, grp].astype(F32)
        return carry

    with jax.named_scope("third"):
        lax.fori_loop(0, PB, third, 0)

    def fourth(i, carry):
        c3a(i).wait_recv()
        u = k3[i, :, :WA] + r3a[i].astype(F32)
        v = k3[i, :, WA:]
        for d in range(1, G):
            c3b(i, d).wait_recv()
            v = v + r3b[i, d - 1].astype(F32)

        @pl.when(i < PB - 1)
        def _():
            sz[i, :, :WA] = u.astype(BF)
            sz[i, :, WA:] = v.astype(BF)
            c4(i).start()

        @pl.when(i == PB - 1)
        def _():
            out[:, :WA] = u
            out[:, WA:] = v

        return carry

    with jax.named_scope("fourth"):
        lax.fori_loop(0, PB, fourth, 0)

    with jax.named_scope("last"):
        total = out[...]
        for i in range(PB - 1):
            c4(i).wait_recv()
            total = total + rz[i].astype(F32)
        out[...] = total

    for h in range(PH):
        for k in range(HM):
            f_copy(h, other_half(k)).wait_send()
            g_copy(h, other_half(k)).wait_send()
        for k in range(1, HM):
            f_copy(h, same_half(k)).wait_send()
            g_copy(h, same_half(k)).wait_send()
    for i in range(PB):
        c1(i).wait_send()
        for d in range(1, G):
            c2a(i, d).wait_send()
            c3b(i, d).wait_send()
        c2b(i).wait_send()
        c3a(i).wait_send()
        if i < PB - 1:
            c4(i).wait_send()


def split(res, out_in, out_out):
    H = out_in.shape[1]
    out_in[...] = res[:, :H]
    out_out[...] = res[:, H : H + out_out.shape[1]]


def per_device(latent, w_in, w_out, target, cell_mask):
    M = lax.axis_size("member")
    CN = lax.axis_size("cell")
    N, D = latent.shape[1:]
    H = w_in.shape[1]
    FD = w_out.shape[1]
    PH = PHASES
    C = N // M
    CH = C // PH
    K = M * CH
    PB, G = M // 2, CN // 2
    n = FD // (LANES - FD)
    PR = CH // (n + 1) * n
    r = D // (M * CN)
    W = H + LANES
    WA = (W // LANES + 1) // 2 * LANES
    WB = W - WA
    NB = -(-(LANES - math.gcd(C, LANES) + C) // LANES)
    GS = max(G - 1, 1)
    V = pltpu.VMEM
    DMA = pltpu.SemaphoreType.DMA
    vm = pl.BlockSpec(memory_space=pltpu.VMEM)
    res = pl.pallas_call(
        functools.partial(body, M, CN, WA),
        out_shape=jax.ShapeDtypeStruct((r, W), F32),
        in_specs=[pl.BlockSpec(memory_space=pl.ANY)] * 5,
        out_specs=vm,
        scratch_shapes=[
            V((2 * PH, M // 2, CH, D), BF), V((D, H), BF), V((LANES, H), BF), V((FD, N), BF), V((N,), jnp.int32),
            V((N, H), F32), V((N, H), BF), V((N, H), BF), V((N, LANES), BF), V((PH, D, K), BF), V((PH, H, K), BF),
            V((NB * LANES, LANES), F32), V((N, 8), F32),
            V((PH, M, PR, LANES), BF), V((PH, M, PR, LANES), BF), V((PH, M, PR, LANES), BF), V((PH, M, PR, LANES), BF),
            V((PB, 2 * CN * r, W), F32), V((PB, 2, 2, G, r, W), F32), V((PB, 2, 2, G, r, W), BF), V((PB, 2, G, r, W), BF),
            V((PB, 2, G, r, W), F32), V((PB, G, 2, r, WA), BF), V((PB, 2, G, r, WB), BF),
            V((PB, GS, 2, r, WA), BF), V((PB, G, r, WB), BF),
            V((PB, r, W), F32), V((PB, r, WA), BF), V((PB, G, r, WB), BF), V((PB, r, WA), BF), V((PB, GS, r, WB), BF),
            V((PB, r, W), BF), V((PB, r, W), BF),
            DMA((2 * PH + 4,)), DMA((PH, M)), DMA((PH, M)), DMA((PH, M)), DMA((PH, M)),
            DMA((PB,)), DMA((PB,)), DMA((PB, GS)), DMA((PB, GS)), DMA((PB,)), DMA((PB,)),
            DMA((PB,)), DMA((PB,)), DMA((PB, GS)), DMA((PB, GS)), DMA((PB,)), DMA((PB,)),
        ],
        compiler_params=pltpu.CompilerParams(
            collective_id=0, has_side_effects=True, vmem_limit_bytes=60 * 1024 * 1024
        ),
    )(latent.reshape(M, C, D), w_in, w_out.T, target, cell_mask)
    return pl.pallas_call(
        split,
        out_shape=(jax.ShapeDtypeStruct((r, H), F32), jax.ShapeDtypeStruct((r, FD), F32)),
        in_specs=[vm],
        out_specs=(vm, vm),
    )(res)


def solution(mesh):
    in_specs = (P("member", "cell", None), P(), P(), P(None, "cell"), P("cell"))
    out_specs = (P(("member", "cell"), None), P(("member", "cell"), None))
    return jax.shard_map(
        per_device, mesh=mesh, in_specs=in_specs, out_specs=out_specs, check_vma=False
    )
```

```python
import functools
import math

import jax
import jax.numpy as jnp
from jax import lax
from jax.experimental import pallas as pl
from jax.experimental.pallas import tpu as pltpu
from jax.sharding import PartitionSpec as P

MESH = pl.DeviceIdType.MESH
BF = jnp.bfloat16
F32 = jnp.float32
LANES = 128
PHASES = 3


def smooth(d):
    return d * lax.rsqrt(1.0 + d * d)


def mm(a, b):
    return jnp.dot(a, b, preferred_element_type=F32)


def pack(f, width):
    spare = LANES - width
    n = width // spare
    q = f.shape[0] // (n + 1)
    lane = lax.broadcasted_iota(jnp.int32, (q, LANES), 1)
    last = f[n * q :]
    parts = []
    for k in range(n):
        parts.append(jnp.where(lane < width, f[k * q : (k + 1) * q], pltpu.roll(last, width - spare * k, 1)))
    return jnp.concatenate(parts, axis=0)


def unpack_last(p, width):
    spare = LANES - width
    n = width // spare
    q = p.shape[0] // n
    lane = lax.broadcasted_iota(jnp.int32, (q, LANES), 1)
    out = pltpu.roll(p[:q], spare, 1)
    for k in range(1, n):
        out = jnp.where(lane < spare * k, out, pltpu.roll(p[k * q : (k + 1) * q], spare * (k + 1), 1))
    return out


def body(
    M, CN, chunks,
    lat_hbm, w_in_hbm, w_out_hbm, target_hbm, mask_hbm, out_in, out_out,
    lat, w_in, wo, wh, target, mask, slope, hid, gp, gfu, lat_t, hid_t, tgt_t, wgt_t,
    fsend, frecv, gsend, gf,
    acc, kf, sb, r1, s2, r2a, r2b, k3, s3a, r3a, s3b, r3b, sz, rz,
    sem_in, sem_fs, sem_fr, sem_gs, sem_gr,
    sem1s, sem1r, sem2as, sem2ar, sem2bs, sem2br, sem3as, sem3ar, sem3bs, sem3br, sem4s, sem4r,
):
    me = lax.axis_index("member")
    cell = lax.axis_index("cell")
    core = lax.rem(cell, 2)
    grp = cell // 2
    G = CN // 2
    HM = M // 2
    PB = M // 2
    z = me // 2
    x = lax.rem(me, 2)
    half = me // HM
    near, far = half * HM, (1 - half) * HM
    PH = fsend.shape[0]
    CH, D = lat.shape[2:]
    H = w_in.shape[1]
    FD = w_out_hbm.shape[0]
    B = HM * CH
    K = M * CH
    C = PH * CH
    N = PH * K
    PR = fsend.shape[2]
    W = acc.shape[2]
    r = D // (M * CN)
    scale = 1.0 / (float(N * CN) ** 0.5) / M
    pair_core = (me, grp * 2 + 1 - core)
    pair_x = (me + 1 - 2 * x, cell)

    barrier = pltpu.get_barrier_semaphore()
    for d in range(1, M):
        pl.semaphore_signal(barrier, inc=1, device_id=(lax.rem(me + d, M), cell), device_id_type=MESH)
    pl.semaphore_signal(barrier, inc=1, device_id=pair_core, device_id_type=MESH)
    for d in range(1, G):
        pl.semaphore_signal(
            barrier, inc=1, device_id=(me, lax.rem(grp + d, G) * 2 + core), device_id_type=MESH
        )

    def load(rel, h):
        return pltpu.make_async_copy(
            lat_hbm.at[pl.ds(near if rel else far, HM), pl.ds(h * CH, CH), :],
            lat.at[rel * PH + h],
            sem_in.at[rel * PH + h],
        )

    load_w = pltpu.make_async_copy(w_in_hbm, w_in, sem_in.at[2 * PH])
    load_o = pltpu.make_async_copy(w_out_hbm, wo.at[pl.ds(0, FD), :], sem_in.at[2 * PH + 1])
    load_t = pltpu.make_async_copy(target_hbm, target, sem_in.at[2 * PH + 2])
    load_m = pltpu.make_async_copy(mask_hbm, mask, sem_in.at[2 * PH + 3])
    load_w.start()
    load(0, 0).start()
    load_o.start()
    for i in range(1, 2 * PH):
        load(i // PH, i % PH).start()
    load_t.start()
    load_m.start()
    wo[FD:, :] = jnp.zeros((LANES - FD, H), BF)

    def f_copy(h, t):
        return pltpu.make_async_remote_copy(
            fsend.at[h, t], frecv.at[h, me], sem_fs.at[0], sem_fr.at[h],
            device_id=(t, cell), device_id_type=MESH,
        )

    def g_copy(h, t, rel):
        return pltpu.make_async_remote_copy(
            gsend.at[h, t], gf.at[h, me], sem_gs.at[0], sem_gr.at[rel, h],
            device_id=(t, cell), device_id_type=MESH,
        )

    def arrived(ref, sem):
        pltpu.make_async_copy(ref, ref, sem).wait()

    def same_half(k):
        return near + lax.rem(me + k, HM)

    def c1(i):
        return pltpu.make_async_remote_copy(
            sb.at[i], r1.at[i], sem1s.at[0], sem1r.at[i], device_id=pair_core, device_id_type=MESH
        )

    def c2a(i, q, d):
        cols = pl.ds(chunks[q][0], chunks[q][1] - chunks[q][0])
        g = lax.rem(grp + d, G)
        return pltpu.make_async_remote_copy(
            s2.at[i, :, g, :, cols], r2a.at[i, d - 1, :, :, cols], sem2as.at[0], sem2ar.at[q, i, d - 1],
            device_id=(me, g * 2 + core), device_id_type=MESH,
        )

    def c2b(i, q):
        cols = pl.ds(chunks[q][1], chunks[q][2] - chunks[q][1])
        return pltpu.make_async_remote_copy(
            s2.at[i, 1 - x, :, :, cols], r2b.at[i, :, :, cols], sem2bs.at[0], sem2br.at[q, i],
            device_id=pair_x, device_id_type=MESH,
        )

    def c3a(i, q):
        cols = pl.ds(chunks[q][0], chunks[q][1] - chunks[q][0])
        return pltpu.make_async_remote_copy(
            s3a.at[i, :, cols], r3a.at[i, :, cols], sem3as.at[0], sem3ar.at[q, i],
            device_id=pair_x, device_id_type=MESH,
        )

    def c3b(i, q, d):
        cols = pl.ds(chunks[q][1], chunks[q][2] - chunks[q][1])
        g = lax.rem(grp + d, G)
        return pltpu.make_async_remote_copy(
            s3b.at[i, g, :, cols], r3b.at[i, d - 1, :, cols], sem3bs.at[0], sem3br.at[q, i, d - 1],
            device_id=(me, g * 2 + core), device_id_type=MESH,
        )

    HP = PB // 2
    zh = z // HP

    def block_of(i):
        far = (1 - zh) * HP + lax.rem(z + i + 1, HP)
        near = zh * HP + lax.rem(z + i + 1, HP)
        return jnp.where(i < HP, far, near)

    def c4(i, q):
        cols = pl.ds(chunks[q][0], chunks[q][2] - chunks[q][0])
        return pltpu.make_async_remote_copy(
            sz.at[i, :, cols], rz.at[i, :, cols], sem4s.at[0], sem4r.at[0],
            device_id=(block_of(i) * 2 + x, cell), device_id_type=MESH,
        )

    def decode(rel, h0, blocks):
        at = rel * PH + h0
        rows = slice(at * B, (at + blocks) * B)
        for h in range(h0, h0 + blocks):
            load(rel, h).wait()
        v = mm(lat[at : at + blocks].reshape(blocks * B, D), w_in[...])
        u = 0.5 * v
        t = jnp.tanh(u)
        ut = u * t
        hb = (u + ut).astype(BF)
        slope[rows, :] = (1.0 + t) + (u - ut * t)
        hid[rows, :] = hb
        return lax.dot_general(hb, wo[...], (((1,), (1,)), ((), ())), preferred_element_type=F32)

    def send_fields(rel, h0, blocks, f):
        for h in range(h0, h0 + blocks):
            for k in range(HM):
                at = ((h - h0) * HM + k) * CH
                t = (near if rel else far) + k
                fsend[h, t] = pack(f[at : at + CH], FD).astype(BF)
                if not rel:
                    f_copy(h, t).start()
            if rel:
                frecv[h, me] = fsend[h, me]
                for k in range(1, HM):
                    f_copy(h, same_half(k)).start()

    with jax.named_scope("forward"):
        load_w.wait()
        load_o.wait()
        f = decode(0, 0, 1)
        pl.semaphore_wait(barrier, M - 1 + 1 + G - 1)
        send_fields(0, 0, 1, f)
        send_fields(0, 1, PH - 1, decode(0, 1, PH - 1))
        send_fields(1, 0, 1, decode(1, 0, 1))
        send_fields(1, 1, PH - 1, decode(1, 1, PH - 1))

    with jax.named_scope("prep"):
        load_t.wait()
        load_m.wait()
        wh[...] = (0.5 * wo[...].astype(F32)).astype(BF)
        NB = tgt_t.shape[0] // LANES
        b0 = jnp.minimum(me * C // LANES, N // LANES - NB)
        for b in range(NB):
            cols = pl.ds(pl.multiple_of((b0 + b) * LANES, LANES), LANES)
            tgt_t[b * LANES : (b + 1) * LANES, :FD] = target[:, cols].astype(F32).T
        for b in range(N // LANES):
            cols = slice(LANES * b, LANES * b + LANES)
            w = mask[cols].astype(F32) * scale
            wgt_t[cols, :] = jnp.broadcast_to(w[None, :], (8, LANES)).T

    RB = 16 if PR % 16 == 0 else PR

    def phase(h, carry):
        arrived(frecv.at[h, pl.ds(0, M - 1)], sem_fr.at[h])
        own = pl.multiple_of(me * C - b0 * LANES + h * CH, 8)
        tp = pack(tgt_t[pl.ds(own, CH), :], FD)
        wp = pack(
            jnp.broadcast_to(wgt_t[pl.ds(pl.multiple_of(me * C + h * CH, 8), CH), 0:1], (CH, LANES)), FD
        )
        for b in range(PR // RB):
            rows = slice(b * RB, (b + 1) * RB)
            vals = [frecv[h, j, rows, :].astype(F32) for j in range(M)]
            total = [None] * M
            for a in range(M):
                for c in range(a + 1, M):
                    k = smooth(vals[a] - vals[c])
                    total[a] = k if total[a] is None else total[a] + k
                    total[c] = -k if total[c] is None else total[c] - k
            for a in range(M):
                g = wp[rows] * (smooth(vals[a] - tp[rows]) - total[a] * (1.0 / M))
                gsend[h, a, rows, :] = g.astype(BF)
        for k in range(HM):
            g_copy(h, far + k, 0).start()
        for k in range(1, HM):
            g_copy(h, same_half(k), 1).start()
        gf[h, me] = gsend[h, me]
        for b in range(K // LANES):
            rel, at = b * LANES // B, b * LANES % B
            cols = slice(LANES * b, LANES * b + LANES)
            lat_t[h, :, cols] = lat[rel * PH + h].reshape(B, D)[at : at + LANES, :].T
            hid_t[h, :, cols] = hid[pl.ds(pl.multiple_of((rel * PH + h) * B + at, LANES), LANES), :].T
        return carry

    with jax.named_scope("pairs"):
        lax.fori_loop(0, PH, phase, 0)

    def back(h, rel):
        blk = 2 * h + rel
        for k in range(HM):
            p = gf[h, (near if rel else far) + k]
            at = pl.multiple_of(blk * B + k * CH, CH)
            gfu[pl.ds(at, PR), :] = p
            gfu[pl.ds(pl.multiple_of(at + PR, CH - PR), CH - PR), :] = unpack_last(p.astype(F32), FD).astype(BF)
        rows = pl.ds(pl.multiple_of(blk * B, B), B)
        held = pl.ds(pl.multiple_of((rel * PH + h) * B, B), B)
        gp[rows, :] = (mm(gfu[rows, :], wh[...]) * slope[held, :]).astype(BF)

    def gather(h):
        arrived(gf.at[h, pl.ds(0, HM - 1)], sem_gr.at[1, h])
        back(h, 1)
        arrived(gf.at[h, pl.ds(0, HM)], sem_gr.at[0, h])
        back(h, 0)

    def terms(h, p):
        rows = pl.ds(pl.multiple_of(p * (2 * r * CN), 2 * r * CN), 2 * r * CN)
        at = pl.ds(pl.multiple_of(h * K, K), K)
        return mm(lat_t[h, rows, :], gp[at, :]), mm(hid_t[h, rows, :], gfu[at, :])

    def early(h, carry):
        gather(h)

        def add(p, c):
            a, b = terms(h, p)

            @pl.when(h == 0)
            def _():
                acc[p, :, :H] = a
                acc[p, :, H:] = b

            @pl.when(h > 0)
            def _():
                acc[p, :, :H] += a
                acc[p, :, H:] += b

            return c

        return lax.fori_loop(0, PB, add, carry)

    with jax.named_scope("early"):
        lax.fori_loop(0, PH - 1, early, 0)

    with jax.named_scope("gather"):
        gather(PH - 1)

    def first(i):
        p = block_of(i)
        a, b = terms(PH - 1, p)
        v = jnp.concatenate([a + acc[p, :, :H], b + acc[p, :, H:]], axis=1)
        for s in range(2):
            for g in range(G):
                at = (s * CN + 2 * g) * r
                low, high = v[at : at + r], v[at + r : at + 2 * r]
                sb[i, s, g] = jnp.where(core == 0, high, low).astype(BF)
                kf[i, s, g] = jnp.where(core == 0, low, high)
        c1(i).start()

    def start_second(i, q):
        for d in range(1, G):
            c2a(i, q, d).start()
        c2b(i, q).start()

    def second(i):
        c1(i).wait_recv()
        for s in range(2):
            for g in range(G):
                v = kf[i, s, g] + r1[i, s, g].astype(F32)
                kf[i, s, g] = v
                s2[i, s, g] = v.astype(BF)

        @pl.when(i < 2)
        def _():
            for q in range(NQ):
                start_second(i, q)

    NQ = len(chunks)

    def opening(i, carry):
        @pl.when(i < PB)
        def _():
            first(i)

        @pl.when(i >= 2)
        def _():
            second(i - 2)

        return carry

    with jax.named_scope("opening"):
        lax.fori_loop(0, PB + 2, opening, 0)

    def third(i, q):
        a0, a1, b1 = chunks[q]
        for d in range(1, G):
            c2a(i, q, d).wait_recv()
        away = kf[i, 1 - x, grp, :, a0:a1]
        keep = kf[i, x, grp, :, a0:a1]
        for d in range(1, G):
            away = away + r2a[i, d - 1, 1 - x, :, a0:a1].astype(F32)
            keep = keep + r2a[i, d - 1, x, :, a0:a1].astype(F32)
        s3a[i, :, a0:a1] = away.astype(BF)
        c3a(i, q).start()
        k3[i, :, a0:a1] = keep
        c2b(i, q).wait_recv()
        for g in range(G):
            s3b[i, g, :, a1:b1] = (kf[i, x, g, :, a1:b1] + r2b[i, g, :, a1:b1].astype(F32)).astype(BF)
        for d in range(1, G):
            c3b(i, q, d).start()
        k3[i, :, a1:b1] = kf[i, x, grp, :, a1:b1] + r2b[i, grp, :, a1:b1].astype(F32)

        @pl.when(i + 2 < PB)
        def _():
            start_second(i + 2, q)

    def fourth(i, q):
        a0, a1, b1 = chunks[q]
        c3a(i, q).wait_recv()
        u = k3[i, :, a0:a1] + r3a[i, :, a0:a1].astype(F32)
        v = k3[i, :, a1:b1]
        for d in range(1, G):
            c3b(i, q, d).wait_recv()
            v = v + r3b[i, d - 1, :, a1:b1].astype(F32)

        @pl.when(i < PB - 1)
        def _():
            sz[i, :, a0:a1] = u.astype(BF)
            sz[i, :, a1:b1] = v.astype(BF)
            c4(i, q).start()

        @pl.when(i == PB - 1)
        def _():
            k3[i, :, a0:a1] = u
            k3[i, :, a1:b1] = v

    def stages(i, carry):
        for q in range(NQ):
            @pl.when(i >= 2)
            def _():
                fourth(i - 2, q)

            @pl.when(i < PB)
            def _():
                third(i, q)

        return carry

    with jax.named_scope("stages"):
        lax.fori_loop(0, PB + 2, stages, 0)

    with jax.named_scope("last"):
        total = k3[PB - 1]
        arrived(rz.at[pl.ds(0, PB - 1)], sem4r.at[0])
        for i in range(PB - 1):
            total = total + rz[i].astype(F32)
        out_in[...] = total[:, :H]
        out_out[...] = total[:, H : H + FD]

    arrived(fsend.at[:, pl.ds(0, M - 1)], sem_fs.at[0])
    arrived(gsend.at[:, pl.ds(0, M - 1)], sem_gs.at[0])
    arrived(sb, sem1s.at[0])
    wide = pl.ds(0, sum(c[1] - c[0] for c in chunks))
    narrow = pl.ds(0, sum(c[2] - c[1] for c in chunks))
    arrived(s2.at[:, :, pl.ds(0, G - 1), :, wide], sem2as.at[0])
    arrived(s2.at[:, 0, :, :, narrow], sem2bs.at[0])
    arrived(s3a.at[:, :, wide], sem3as.at[0])
    arrived(s3b.at[:, pl.ds(0, G - 1), :, narrow], sem3bs.at[0])
    arrived(sz.at[pl.ds(0, PB - 1)], sem4s.at[0])


def publish(res_in, res_out, out_in, out_out, sem):
    a = pltpu.make_async_copy(res_in, out_in, sem.at[0])
    b = pltpu.make_async_copy(res_out, out_out, sem.at[1])
    a.start()
    b.start()
    a.wait()
    b.wait()


def per_device(latent, w_in, w_out, target, cell_mask):
    M = lax.axis_size("member")
    CN = lax.axis_size("cell")
    N, D = latent.shape[1:]
    H = w_in.shape[1]
    FD = w_out.shape[1]
    PH = PHASES
    C = N // M
    CH = C // PH
    K = M * CH
    PB, G = M // 2, CN // 2
    n = FD // (LANES - FD)
    PR = CH // (n + 1) * n
    r = D // (M * CN)
    W = H + LANES
    T = W // LANES
    chunks, at = [], 0
    for tiles in ((T + 1) // 2, T // 2):
        chunks.append((at * LANES, (at + (tiles + 1) // 2) * LANES, (at + tiles) * LANES))
        at += tiles
    NQ = len(chunks)
    NB = -(-(LANES - math.gcd(C, LANES) + C) // LANES)
    GS = max(G - 1, 1)
    V = pltpu.VMEM
    DMA = pltpu.SemaphoreType.DMA
    vm = pl.BlockSpec(memory_space=pltpu.VMEM)
    res = pl.pallas_call(
        functools.partial(body, M, CN, tuple(chunks)),
        out_shape=(V((r, H), F32), V((r, FD), F32)),
        in_specs=[pl.BlockSpec(memory_space=pl.ANY)] * 5,
        out_specs=(vm, vm),
        scratch_shapes=[
            V((2 * PH, M // 2, CH, D), BF), V((D, H), BF), V((LANES, H), BF), V((LANES, H), BF),
            V((FD, N), BF), V((N,), jnp.int32),
            V((N, H), F32), V((N, H), BF), V((N, H), BF), V((N, LANES), BF), V((PH, D, K), BF), V((PH, H, K), BF),
            V((NB * LANES, LANES), F32), V((N, 8), F32),
            V((PH, M, PR, LANES), BF), V((PH, M, PR, LANES), BF), V((PH, M, PR, LANES), BF), V((PH, M, PR, LANES), BF),
            V((PB, 2 * CN * r, W), F32), V((PB, 2, G, r, W), F32), V((PB, 2, G, r, W), BF), V((PB, 2, G, r, W), BF),
            V((PB, 2, G, r, W), BF), V((PB, GS, 2, r, W), BF), V((PB, G, r, W), BF),
            V((PB, r, W), F32), V((PB, r, W), BF), V((PB, r, W), BF), V((PB, G, r, W), BF), V((PB, GS, r, W), BF),
            V((PB, r, W), BF), V((PB, r, W), BF),
            DMA((2 * PH + 4,)), DMA((1,)), DMA((PH,)), DMA((1,)), DMA((2, PH)),
            DMA((1,)), DMA((PB,)), DMA((1,)), DMA((NQ, PB, GS)), DMA((1,)), DMA((NQ, PB)),
            DMA((1,)), DMA((NQ, PB)), DMA((1,)), DMA((NQ, PB, GS)), DMA((1,)), DMA((1,)),
        ],
        compiler_params=pltpu.CompilerParams(
            collective_id=0, has_side_effects=True, vmem_limit_bytes=60 * 1024 * 1024
        ),
    )(latent.reshape(M, C, D), w_in, w_out.T, target, cell_mask)
    return pl.pallas_call(
        publish,
        out_shape=(jax.ShapeDtypeStruct((r, H), F32), jax.ShapeDtypeStruct((r, FD), F32)),
        in_specs=[vm, vm],
        out_specs=(pl.BlockSpec(memory_space=pl.ANY),) * 2,
        scratch_shapes=[DMA((2,))],
        compiler_params=pltpu.CompilerParams(vmem_limit_bytes=1024 * 1024),
    )(*(pltpu.with_memory_space_constraint(o, pltpu.VMEM) for o in res))


def solution(mesh):
    in_specs = (P("member", "cell", None), P(), P(), P(None, "cell"), P("cell"))
    out_specs = (P(("member", "cell"), None), P(("member", "cell"), None))
    return jax.shard_map(
        per_device, mesh=mesh, in_specs=in_specs, out_specs=out_specs, check_vma=False
    )
```

```python
import functools
import math

import jax
import jax.numpy as jnp
from jax import lax
from jax.experimental import pallas as pl
from jax.experimental.pallas import tpu as pltpu
from jax.sharding import PartitionSpec as P

MESH = pl.DeviceIdType.MESH
BF = jnp.bfloat16
F32 = jnp.float32
LANES = 128
PHASES = 3


def smooth(d):
    return d * lax.rsqrt(1.0 + d * d)


def mm(a, b):
    return jnp.dot(a, b, preferred_element_type=F32)


def pack(f, width):
    spare = LANES - width
    n = width // spare
    q = f.shape[0] // (n + 1)
    lane = lax.broadcasted_iota(jnp.int32, (q, LANES), 1)
    last = f[n * q :]
    parts = []
    for k in range(n):
        parts.append(jnp.where(lane < width, f[k * q : (k + 1) * q], pltpu.roll(last, width - spare * k, 1)))
    return jnp.concatenate(parts, axis=0)


def unpack_last(p, width):
    spare = LANES - width
    n = width // spare
    q = p.shape[0] // n
    lane = lax.broadcasted_iota(jnp.int32, (q, LANES), 1)
    out = pltpu.roll(p[:q], spare, 1)
    for k in range(1, n):
        out = jnp.where(lane < spare * k, out, pltpu.roll(p[k * q : (k + 1) * q], spare * (k + 1), 1))
    return out


def body(
    M, CN, chunks,
    lat_hbm, w_in_hbm, w_out_hbm, target_hbm, mask_hbm, out_in, out_out,
    lat, w_in, wo, wh, target, mask, slope, hid, gp, gfu, lat_t, hid_t, tgt_t, wgt_t,
    fsend, frecv, gsend, gf,
    acc, kf, sb, r1, s2, r2a, r2b, k3, s3a, r3a, s3b, r3b, sz, rz,
    sem_in, sem_fs, sem_fr, sem_gs, sem_gr,
    sem1s, sem1r, sem2as, sem2ar, sem2bs, sem2br, sem3as, sem3ar, sem3bs, sem3br, sem4s, sem4r,
):
    me = lax.axis_index("member")
    cell = lax.axis_index("cell")
    core = lax.rem(cell, 2)
    grp = cell // 2
    G = CN // 2
    HM = M // 2
    PB = M // 2
    z = me // 2
    x = lax.rem(me, 2)
    half = me // HM
    near, far = half * HM, (1 - half) * HM
    PH = fsend.shape[0]
    CH, D = lat.shape[2:]
    H = w_in.shape[1]
    FD = w_out_hbm.shape[0]
    B = HM * CH
    K = M * CH
    C = PH * CH
    N = PH * K
    PR = fsend.shape[2]
    W = acc.shape[2]
    r = D // (M * CN)
    scale = 1.0 / (float(N * CN) ** 0.5) / M
    pair_core = (me, grp * 2 + 1 - core)
    pair_x = (me + 1 - 2 * x, cell)

    barrier = pltpu.get_barrier_semaphore()
    for d in range(1, M):
        pl.semaphore_signal(barrier, inc=1, device_id=(lax.rem(me + d, M), cell), device_id_type=MESH)
    pl.semaphore_signal(barrier, inc=1, device_id=pair_core, device_id_type=MESH)
    for d in range(1, G):
        pl.semaphore_signal(
            barrier, inc=1, device_id=(me, lax.rem(grp + d, G) * 2 + core), device_id_type=MESH
        )

    def load(rel, h):
        return pltpu.make_async_copy(
            lat_hbm.at[pl.ds(near if rel else far, HM), pl.ds(h * CH, CH), :],
            lat.at[rel * PH + h],
            sem_in.at[rel * PH + h],
        )

    load_w = pltpu.make_async_copy(w_in_hbm, w_in, sem_in.at[2 * PH])
    load_o = pltpu.make_async_copy(w_out_hbm, wo.at[pl.ds(0, FD), :], sem_in.at[2 * PH + 1])
    load_t = pltpu.make_async_copy(target_hbm, target, sem_in.at[2 * PH + 2])
    load_m = pltpu.make_async_copy(mask_hbm, mask, sem_in.at[2 * PH + 3])
    load_t.start()
    load_m.start()
    load_w.start()
    load(0, 0).start()
    load_o.start()
    for i in range(1, 2 * PH):
        load(i % 2, i // 2).start()
    wo[FD:, :] = jnp.zeros((LANES - FD, H), BF)

    def f_copy(h, t):
        return pltpu.make_async_remote_copy(
            fsend.at[h, t], frecv.at[h, me], sem_fs.at[0], sem_fr.at[h],
            device_id=(t, cell), device_id_type=MESH,
        )

    def g_copy(h, t, rel):
        return pltpu.make_async_remote_copy(
            gsend.at[h, t], gf.at[h, me], sem_gs.at[0], sem_gr.at[rel, h],
            device_id=(t, cell), device_id_type=MESH,
        )

    def arrived(ref, sem):
        pltpu.make_async_copy(ref, ref, sem).wait()

    def same_half(k):
        return near + lax.rem(me + k, HM)

    def c1(i):
        return pltpu.make_async_remote_copy(
            sb.at[i], r1.at[i], sem1s.at[0], sem1r.at[i], device_id=pair_core, device_id_type=MESH
        )

    def c2a(i, q, d):
        cols = pl.ds(chunks[q][0], chunks[q][1] - chunks[q][0])
        g = lax.rem(grp + d, G)
        return pltpu.make_async_remote_copy(
            s2.at[i, :, g, :, cols], r2a.at[i, d - 1, :, :, cols], sem2as.at[0], sem2ar.at[q, i, d - 1],
            device_id=(me, g * 2 + core), device_id_type=MESH,
        )

    def c2b(i, q):
        cols = pl.ds(chunks[q][1], chunks[q][2] - chunks[q][1])
        return pltpu.make_async_remote_copy(
            s2.at[i, 1 - x, :, :, cols], r2b.at[i, :, :, cols], sem2bs.at[0], sem2br.at[q, i],
            device_id=pair_x, device_id_type=MESH,
        )

    def c3a(i, q):
        cols = pl.ds(chunks[q][0], chunks[q][1] - chunks[q][0])
        return pltpu.make_async_remote_copy(
            s3a.at[i, :, cols], r3a.at[i, :, cols], sem3as.at[0], sem3ar.at[q, i],
            device_id=pair_x, device_id_type=MESH,
        )

    def c3b(i, q, d):
        cols = pl.ds(chunks[q][1], chunks[q][2] - chunks[q][1])
        g = lax.rem(grp + d, G)
        return pltpu.make_async_remote_copy(
            s3b.at[i, g, :, cols], r3b.at[i, d - 1, :, cols], sem3bs.at[0], sem3br.at[q, i, d - 1],
            device_id=(me, g * 2 + core), device_id_type=MESH,
        )

    HP = PB // 2
    zh = z // HP

    def block_of(i):
        far = (1 - zh) * HP + lax.rem(z + i + 1, HP)
        near = zh * HP + lax.rem(z + i + 1, HP)
        return jnp.where(i < HP, far, near)

    def c4(i, q):
        cols = pl.ds(chunks[q][0], chunks[q][2] - chunks[q][0])
        return pltpu.make_async_remote_copy(
            sz.at[i, :, cols], rz.at[i, :, cols], sem4s.at[0], sem4r.at[0],
            device_id=(block_of(i) * 2 + x, cell), device_id_type=MESH,
        )

    def decode(rel, h):
        at = rel * PH + h
        rows = slice(at * B, (at + 1) * B)
        load(rel, h).wait()
        v = mm(lat[at].reshape(B, D), w_in[...])
        u = 0.5 * v
        t = jnp.tanh(u)
        ut = u * t
        hb = (u + ut).astype(BF)
        slope[rows, :] = (1.0 + t) + (u - ut * t)
        hid[rows, :] = hb
        return lax.dot_general(hb, wo[...], (((1,), (1,)), ((), ())), preferred_element_type=F32)

    def send_fields(rel, h, f):
        for k in range(HM):
            t = (near if rel else far) + k
            fsend[h, t] = pack(f[k * CH : (k + 1) * CH], FD).astype(BF)
            if not rel:
                f_copy(h, t).start()
        if rel:
            frecv[h, me] = fsend[h, me]
            for k in range(1, HM):
                f_copy(h, same_half(k)).start()

    with jax.named_scope("prep"):
        load_t.wait()
        load_m.wait()
        NB = tgt_t.shape[0] // LANES
        b0 = jnp.minimum(me * C // LANES, N // LANES - NB)
        for b in range(NB):
            cols = pl.ds(pl.multiple_of((b0 + b) * LANES, LANES), LANES)
            tgt_t[b * LANES : (b + 1) * LANES, :FD] = target[:, cols].astype(F32).T
        for b in range(N // LANES):
            cols = slice(LANES * b, LANES * b + LANES)
            w = mask[cols].astype(F32) * scale
            wgt_t[cols, :] = jnp.broadcast_to(w[None, :], (8, LANES)).T

    with jax.named_scope("forward"):
        load_w.wait()
        load_o.wait()
        f = decode(0, 0)
        pl.semaphore_wait(barrier, M - 1 + 1 + G - 1)
        send_fields(0, 0, f)
        for i in range(1, 2 * PH):
            send_fields(i % 2, i // 2, decode(i % 2, i // 2))
        wh[...] = (0.5 * wo[...].astype(F32)).astype(BF)

    RB = 16 if PR % 16 == 0 else PR

    def phase(h, carry):
        arrived(frecv.at[h, pl.ds(0, M - 1)], sem_fr.at[h])
        own = pl.multiple_of(me * C - b0 * LANES + h * CH, 8)
        tp = pack(tgt_t[pl.ds(own, CH), :], FD)
        wp = pack(
            jnp.broadcast_to(wgt_t[pl.ds(pl.multiple_of(me * C + h * CH, 8), CH), 0:1], (CH, LANES)), FD
        )
        for b in range(PR // RB):
            rows = slice(b * RB, (b + 1) * RB)
            vals = [frecv[h, j, rows, :].astype(F32) for j in range(M)]
            total = [None] * M
            for a in range(M):
                for c in range(a + 1, M):
                    k = smooth(vals[a] - vals[c])
                    total[a] = k if total[a] is None else total[a] + k
                    total[c] = -k if total[c] is None else total[c] - k
            for a in range(M):
                g = wp[rows] * (smooth(vals[a] - tp[rows]) - total[a] * (1.0 / M))
                gsend[h, a, rows, :] = g.astype(BF)
        for k in range(HM):
            g_copy(h, far + k, 0).start()
        for k in range(1, HM):
            g_copy(h, same_half(k), 1).start()
        gf[h, me] = gsend[h, me]
        for b in range(K // LANES):
            rel, at = b * LANES // B, b * LANES % B
            cols = pl.ds(pl.multiple_of(h * K + LANES * b, LANES), LANES)
            lat_t[:, cols] = lat[rel * PH + h].reshape(B, D)[at : at + LANES, :].T
            hid_t[:, cols] = hid[pl.ds(pl.multiple_of((rel * PH + h) * B + at, LANES), LANES), :].T
        return carry

    with jax.named_scope("pairs"):
        lax.fori_loop(0, PH, phase, 0)

    def back(h, rel):
        blk = 2 * h + rel
        for k in range(HM):
            p = gf[h, (near if rel else far) + k]
            at = pl.multiple_of(blk * B + k * CH, CH)
            gfu[pl.ds(at, PR), :] = p
            gfu[pl.ds(pl.multiple_of(at + PR, CH - PR), CH - PR), :] = unpack_last(p.astype(F32), FD).astype(BF)
        rows = pl.ds(pl.multiple_of(blk * B, B), B)
        held = pl.ds(pl.multiple_of((rel * PH + h) * B, B), B)
        gp[rows, :] = (mm(gfu[rows, :], wh[...]) * slope[held, :]).astype(BF)

    def gather(h):
        arrived(gf.at[h, pl.ds(0, HM - 1)], sem_gr.at[1, h])
        back(h, 1)
        arrived(gf.at[h, pl.ds(0, HM)], sem_gr.at[0, h])
        back(h, 0)

    def terms(h0, phases, i):
        rows = pl.ds(pl.multiple_of(block_of(i) * (2 * r * CN), 2 * r * CN), 2 * r * CN)
        at = slice(h0 * K, (h0 + phases) * K)
        return jnp.concatenate([mm(lat_t[rows, at], gp[at, :]), mm(hid_t[rows, at], gfu[at, :])], axis=1)

    def early(i, carry):
        acc[i] = terms(0, 1, i)
        return carry

    with jax.named_scope("early"):
        gather(0)
        lax.fori_loop(0, PB, early, 0)
        for h in range(1, PH - 1):
            gather(h)
        acc[0] += terms(1, PH - 2, 0)

    with jax.named_scope("gather"):
        gather(PH - 1)

    def first(i, v):
        v = v + acc[i]
        for s in range(2):
            for g in range(G):
                at = (s * CN + 2 * g) * r
                low, high = v[at : at + r], v[at + r : at + 2 * r]
                sb[i, s, g] = jnp.where(core == 0, high, low).astype(BF)
                kf[i, s, g] = jnp.where(core == 0, low, high)
        c1(i).start()

    def start_second(i, q):
        for d in range(1, G):
            c2a(i, q, d).start()
        c2b(i, q).start()

    def second(i):
        c1(i).wait_recv()
        for s in range(2):
            for g in range(G):
                v = kf[i, s, g] + r1[i, s, g].astype(F32)
                kf[i, s, g] = v
                s2[i, s, g] = v.astype(BF)

        for q in range(2):
            @pl.when(2 * i + q < 5)
            def _():
                start_second(i, q)

    def opening(i, carry):
        @pl.when(i < PB)
        def _():
            first(i, terms(1, PH - 1, i))

        second(i - 1)
        return carry

    with jax.named_scope("opening"):
        first(0, terms(PH - 1, 1, 0))
        lax.fori_loop(1, PB + 1, opening, 0)

    def third(i, q):
        a0, a1, b1 = chunks[q]
        for d in range(1, G):
            c2a(i, q, d).wait_recv()
        away = kf[i, 1 - x, grp, :, a0:a1]
        keep = kf[i, x, grp, :, a0:a1]
        for d in range(1, G):
            away = away + r2a[i, d - 1, 1 - x, :, a0:a1].astype(F32)
            keep = keep + r2a[i, d - 1, x, :, a0:a1].astype(F32)
        s3a[i, :, a0:a1] = away.astype(BF)
        c3a(i, q).start()
        k3[i, :, a0:a1] = keep
        c2b(i, q).wait_recv()
        for g in range(G):
            s3b[i, g, :, a1:b1] = (kf[i, x, g, :, a1:b1] + r2b[i, g, :, a1:b1].astype(F32)).astype(BF)
        for d in range(1, G):
            c3b(i, q, d).start()
        k3[i, :, a1:b1] = kf[i, x, grp, :, a1:b1] + r2b[i, grp, :, a1:b1].astype(F32)

        ahead = i + (5 + q) // 2

        @pl.when(ahead < PB)
        def _():
            start_second(ahead, (5 + q) % 2)

    def fourth(i, q):
        a0, a1, b1 = chunks[q]
        c3a(i, q).wait_recv()
        u = k3[i, :, a0:a1] + r3a[i, :, a0:a1].astype(F32)
        v = k3[i, :, a1:b1]
        for d in range(1, G):
            c3b(i, q, d).wait_recv()
            v = v + r3b[i, d - 1, :, a1:b1].astype(F32)

        @pl.when(i < PB - 1)
        def _():
            sz[i, :, a0:a1] = u.astype(BF)
            sz[i, :, a1:b1] = v.astype(BF)
            c4(i, q).start()

        @pl.when(i == PB - 1)
        def _():
            k3[i, :, a0:a1] = u
            k3[i, :, a1:b1] = v

    def stages(i, carry):
        for q in range(2):
            @pl.when(i < PB)
            def _():
                third(i, q)

            @pl.when(i >= 2)
            def _():
                fourth(i - 2, q)

        return carry

    with jax.named_scope("stages"):
        lax.fori_loop(0, PB + 2, stages, 0)

    with jax.named_scope("last"):
        total = k3[PB - 1]
        arrived(rz.at[pl.ds(0, PB - 1)], sem4r.at[0])
        for i in range(PB - 1):
            total = total + rz[i].astype(F32)
        out_in[...] = total[:, :H]
        out_out[...] = total[:, H : H + FD]

    arrived(fsend.at[:, pl.ds(0, M - 1)], sem_fs.at[0])
    arrived(gsend.at[:, pl.ds(0, M - 1)], sem_gs.at[0])
    arrived(sb, sem1s.at[0])
    wide = pl.ds(0, sum(c[1] - c[0] for c in chunks))
    narrow = pl.ds(0, sum(c[2] - c[1] for c in chunks))
    arrived(s2.at[:, :, pl.ds(0, G - 1), :, wide], sem2as.at[0])
    arrived(s2.at[:, 0, :, :, narrow], sem2bs.at[0])
    arrived(s3a.at[:, :, wide], sem3as.at[0])
    arrived(s3b.at[:, pl.ds(0, G - 1), :, narrow], sem3bs.at[0])
    arrived(sz.at[pl.ds(0, PB - 1)], sem4s.at[0])


def publish(res_in, res_out, out_in, out_out, sem):
    a = pltpu.make_async_copy(res_in, out_in, sem.at[0])
    b = pltpu.make_async_copy(res_out, out_out, sem.at[1])
    a.start()
    b.start()
    a.wait()
    b.wait()


def per_device(latent, w_in, w_out, target, cell_mask):
    M = lax.axis_size("member")
    CN = lax.axis_size("cell")
    N, D = latent.shape[1:]
    H = w_in.shape[1]
    FD = w_out.shape[1]
    PH = PHASES
    C = N // M
    CH = C // PH
    K = M * CH
    PB, G = M // 2, CN // 2
    n = FD // (LANES - FD)
    PR = CH // (n + 1) * n
    r = D // (M * CN)
    W = H + LANES
    T = W // LANES
    chunks, at = [], 0
    for tiles in ((T + 1) // 2, T // 2):
        chunks.append((at * LANES, (at + (tiles + 1) // 2) * LANES, (at + tiles) * LANES))
        at += tiles
    NQ = len(chunks)
    NB = -(-(LANES - math.gcd(C, LANES) + C) // LANES)
    GS = max(G - 1, 1)
    V = pltpu.VMEM
    DMA = pltpu.SemaphoreType.DMA
    vm = pl.BlockSpec(memory_space=pltpu.VMEM)
    res = pl.pallas_call(
        functools.partial(body, M, CN, tuple(chunks)),
        out_shape=(V((r, H), F32), V((r, FD), F32)),
        in_specs=[pl.BlockSpec(memory_space=pl.ANY)] * 5,
        out_specs=(vm, vm),
        scratch_shapes=[
            V((2 * PH, M // 2, CH, D), BF), V((D, H), BF), V((LANES, H), BF), V((LANES, H), BF),
            V((FD, N), BF), V((N,), jnp.int32),
            V((N, H), F32), V((N, H), BF), V((N, H), BF), V((N, LANES), BF), V((D, N), BF), V((H, N), BF),
            V((NB * LANES, LANES), F32), V((N, 8), F32),
            V((PH, M, PR, LANES), BF), V((PH, M, PR, LANES), BF), V((PH, M, PR, LANES), BF), V((PH, M, PR, LANES), BF),
            V((PB, 2 * CN * r, W), F32), V((PB, 2, G, r, W), F32), V((PB, 2, G, r, W), BF), V((PB, 2, G, r, W), BF),
            V((PB, 2, G, r, W), BF), V((PB, GS, 2, r, W), BF), V((PB, G, r, W), BF),
            V((PB, r, W), F32), V((PB, r, W), BF), V((PB, r, W), BF), V((PB, G, r, W), BF), V((PB, GS, r, W), BF),
            V((PB, r, W), BF), V((PB, r, W), BF),
            DMA((2 * PH + 4,)), DMA((1,)), DMA((PH,)), DMA((1,)), DMA((2, PH)),
            DMA((1,)), DMA((PB,)), DMA((1,)), DMA((NQ, PB, GS)), DMA((1,)), DMA((NQ, PB)),
            DMA((1,)), DMA((NQ, PB)), DMA((1,)), DMA((NQ, PB, GS)), DMA((1,)), DMA((1,)),
        ],
        compiler_params=pltpu.CompilerParams(
            collective_id=0, has_side_effects=True, vmem_limit_bytes=60 * 1024 * 1024
        ),
    )(latent.reshape(M, C, D), w_in, w_out.T, target, cell_mask)
    return pl.pallas_call(
        publish,
        out_shape=(jax.ShapeDtypeStruct((r, H), F32), jax.ShapeDtypeStruct((r, FD), F32)),
        in_specs=[vm, vm],
        out_specs=(pl.BlockSpec(memory_space=pl.ANY),) * 2,
        scratch_shapes=[DMA((2,))],
        compiler_params=pltpu.CompilerParams(vmem_limit_bytes=1024 * 1024),
    )(*(pltpu.with_memory_space_constraint(o, pltpu.VMEM) for o in res))


def solution(mesh):
    in_specs = (P("member", "cell", None), P(), P(), P(None, "cell"), P("cell"))
    out_specs = (P(("member", "cell"), None), P(("member", "cell"), None))
    return jax.shard_map(
        per_device, mesh=mesh, in_specs=in_specs, out_specs=out_specs, check_vma=False
    )
```

```python
import functools
import math

import jax
import jax.numpy as jnp
from jax import lax
from jax.experimental import pallas as pl
from jax.experimental.pallas import tpu as pltpu
from jax.sharding import PartitionSpec as P

MESH = pl.DeviceIdType.MESH
BF = jnp.bfloat16
F32 = jnp.float32
LANES = 128
PHASES = 3
AHEAD = 4
BEHIND = 3


def smooth(d):
    return d * lax.rsqrt(1.0 + d * d)


def mm(a, b):
    return jnp.dot(a, b, preferred_element_type=F32)


def pack(f, width):
    spare = LANES - width
    n = width // spare
    q = f.shape[0] // (n + 1)
    lane = lax.broadcasted_iota(jnp.int32, (q, LANES), 1)
    last = f[n * q :]
    parts = []
    for k in range(n):
        parts.append(jnp.where(lane < width, f[k * q : (k + 1) * q], pltpu.roll(last, width - spare * k, 1)))
    return jnp.concatenate(parts, axis=0)


def unpack_last(p, width):
    spare = LANES - width
    n = width // spare
    q = p.shape[0] // n
    lane = lax.broadcasted_iota(jnp.int32, (q, LANES), 1)
    out = pltpu.roll(p[:q], spare, 1)
    for k in range(1, n):
        out = jnp.where(lane < spare * k, out, pltpu.roll(p[k * q : (k + 1) * q], spare * (k + 1), 1))
    return out


def body(
    M, CN, chunks,
    lat_hbm, w_in_hbm, w_out_hbm, target_hbm, mask_hbm, out_in, out_out,
    lat, w_in, wo, wh, target, mask, slope, hid, gp, gfu, lat_t, hid_t, tgt_t, wgt_t,
    fsend, frecv, gsend, gf,
    acc, kf, sb, r1, s2, r2a, r2b, k3, s3a, r3a, s3b, r3b, sz, rz,
    sem_in, sem_fs, sem_fr, sem_gs, sem_gr,
    sem1s, sem1r, sem2as, sem2ar, sem2bs, sem2br, sem3as, sem3ar, sem3bs, sem3br, sem4s, sem4r,
):
    me = lax.axis_index("member")
    cell = lax.axis_index("cell")
    core = lax.rem(cell, 2)
    grp = cell // 2
    G = CN // 2
    HM = M // 2
    PB = M // 2
    z = me // 2
    x = lax.rem(me, 2)
    half = me // HM
    near, far = half * HM, (1 - half) * HM
    PH = fsend.shape[0]
    CH, D = lat.shape[2:]
    H = w_in.shape[1]
    FD = w_out_hbm.shape[0]
    B = HM * CH
    K = M * CH
    C = PH * CH
    N = PH * K
    PR = fsend.shape[2]
    W = acc.shape[2]
    r = D // (M * CN)
    scale = 1.0 / (float(N * CN) ** 0.5) / M
    pair_core = (me, grp * 2 + 1 - core)
    pair_x = (me + 1 - 2 * x, cell)

    barrier = pltpu.get_barrier_semaphore()
    for d in range(1, M):
        pl.semaphore_signal(barrier, inc=1, device_id=(lax.rem(me + d, M), cell), device_id_type=MESH)
    pl.semaphore_signal(barrier, inc=1, device_id=pair_core, device_id_type=MESH)
    for d in range(1, G):
        pl.semaphore_signal(
            barrier, inc=1, device_id=(me, lax.rem(grp + d, G) * 2 + core), device_id_type=MESH
        )

    def load(rel, h):
        return pltpu.make_async_copy(
            lat_hbm.at[pl.ds(near if rel else far, HM), pl.ds(h * CH, CH), :],
            lat.at[rel * PH + h],
            sem_in.at[rel * PH + h],
        )

    load_w = pltpu.make_async_copy(w_in_hbm, w_in, sem_in.at[2 * PH])
    load_o = pltpu.make_async_copy(w_out_hbm, wo.at[pl.ds(0, FD), :], sem_in.at[2 * PH + 1])
    load_t = pltpu.make_async_copy(target_hbm, target, sem_in.at[2 * PH + 2])
    load_m = pltpu.make_async_copy(mask_hbm, mask, sem_in.at[2 * PH + 3])
    load_t.start()
    load_m.start()
    load_w.start()
    load(0, 0).start()
    load_o.start()
    for i in range(1, 2 * PH):
        load(i % 2, i // 2).start()
    wo[FD:, :] = jnp.zeros((LANES - FD, H), BF)

    def f_copy(h, t):
        return pltpu.make_async_remote_copy(
            fsend.at[h, t], frecv.at[h, me], sem_fs.at[0], sem_fr.at[h],
            device_id=(t, cell), device_id_type=MESH,
        )

    def g_copy(h, t, rel):
        return pltpu.make_async_remote_copy(
            gsend.at[h, t], gf.at[h, me], sem_gs.at[0], sem_gr.at[rel, h],
            device_id=(t, cell), device_id_type=MESH,
        )

    def arrived(ref, sem):
        pltpu.make_async_copy(ref, ref, sem).wait()

    def same_half(k):
        return near + lax.rem(me + k, HM)

    def c1(i):
        return pltpu.make_async_remote_copy(
            sb.at[i], r1.at[i], sem1s.at[0], sem1r.at[i], device_id=pair_core, device_id_type=MESH
        )

    def c2a(i, q, d):
        cols = pl.ds(chunks[q][0], chunks[q][1] - chunks[q][0])
        g = lax.rem(grp + d, G)
        return pltpu.make_async_remote_copy(
            s2.at[i, :, g, :, cols], r2a.at[i, d - 1, :, :, cols], sem2as.at[0], sem2ar.at[q, i, d - 1],
            device_id=(me, g * 2 + core), device_id_type=MESH,
        )

    def c2b(i, q):
        cols = pl.ds(chunks[q][1], chunks[q][2] - chunks[q][1])
        return pltpu.make_async_remote_copy(
            s2.at[i, 1 - x, :, :, cols], r2b.at[i, :, :, cols], sem2bs.at[0], sem2br.at[q, i],
            device_id=pair_x, device_id_type=MESH,
        )

    def c3a(i, q):
        cols = pl.ds(chunks[q][0], chunks[q][1] - chunks[q][0])
        return pltpu.make_async_remote_copy(
            s3a.at[i, :, cols], r3a.at[i, :, cols], sem3as.at[0], sem3ar.at[q, i],
            device_id=pair_x, device_id_type=MESH,
        )

    def c3b(i, q, d):
        cols = pl.ds(chunks[q][1], chunks[q][2] - chunks[q][1])
        g = lax.rem(grp + d, G)
        return pltpu.make_async_remote_copy(
            s3b.at[i, g, :, cols], r3b.at[i, d - 1, :, cols], sem3bs.at[0], sem3br.at[q, i, d - 1],
            device_id=(me, g * 2 + core), device_id_type=MESH,
        )

    HP = PB // 2
    zh = z // HP

    def block_of(i):
        far = (1 - zh) * HP + lax.rem(z + i + 1, HP)
        near = zh * HP + lax.rem(z + i + 1, HP)
        return jnp.where(i < HP, far, near)

    def c4(i, q):
        cols = pl.ds(chunks[q][0], chunks[q][2] - chunks[q][0])
        return pltpu.make_async_remote_copy(
            sz.at[i, :, cols], rz.at[i, :, cols], sem4s.at[0], sem4r.at[0],
            device_id=(block_of(i) * 2 + x, cell), device_id_type=MESH,
        )

    def decode(rel, h):
        at = rel * PH + h
        rows = slice(at * B, (at + 1) * B)
        load(rel, h).wait()
        v = mm(lat[at].reshape(B, D), w_in[...])
        u = 0.5 * v
        t = jnp.tanh(u)
        ut = u * t
        hb = (u + ut).astype(BF)
        slope[rows, :] = (1.0 + t) + (u - ut * t)
        hid[rows, :] = hb
        return lax.dot_general(hb, wo[...], (((1,), (1,)), ((), ())), preferred_element_type=F32)

    def send_fields(rel, h, f):
        for k in range(HM):
            t = (near if rel else far) + k
            fsend[h, t] = pack(f[k * CH : (k + 1) * CH], FD).astype(BF)
            if not rel:
                f_copy(h, t).start()
        if rel:
            frecv[h, me] = fsend[h, me]
            for k in range(1, HM):
                f_copy(h, same_half(k)).start()

    with jax.named_scope("prep"):
        load_t.wait()
        load_m.wait()
        NB = tgt_t.shape[0] // LANES
        b0 = jnp.minimum(me * C // LANES, N // LANES - NB)
        for b in range(NB):
            cols = pl.ds(pl.multiple_of((b0 + b) * LANES, LANES), LANES)
            tgt_t[b * LANES : (b + 1) * LANES, :FD] = target[:, cols].astype(F32).T
        for b in range(N // LANES):
            cols = slice(LANES * b, LANES * b + LANES)
            w = mask[cols].astype(F32) * scale
            wgt_t[cols, :] = jnp.broadcast_to(w[None, :], (8, LANES)).T

    with jax.named_scope("forward"):
        load_w.wait()
        load_o.wait()
        f = decode(0, 0)
        pl.semaphore_wait(barrier, M - 1 + 1 + G - 1)
        send_fields(0, 0, f)
        for i in range(1, 2 * PH):
            send_fields(i % 2, i // 2, decode(i % 2, i // 2))
        wh[...] = (0.5 * wo[...].astype(F32)).astype(BF)

    RB = 16 if PR % 16 == 0 else PR

    def phase(h, carry):
        arrived(frecv.at[h, pl.ds(0, M - 1)], sem_fr.at[h])
        own = pl.multiple_of(me * C - b0 * LANES + h * CH, 8)
        tp = pack(tgt_t[pl.ds(own, CH), :], FD)
        wp = pack(
            jnp.broadcast_to(wgt_t[pl.ds(pl.multiple_of(me * C + h * CH, 8), CH), 0:1], (CH, LANES)), FD
        )
        for b in range(PR // RB):
            rows = slice(b * RB, (b + 1) * RB)
            vals = [frecv[h, j, rows, :].astype(F32) for j in range(M)]
            total = [None] * M
            for a in range(M):
                for c in range(a + 1, M):
                    k = smooth(vals[a] - vals[c])
                    total[a] = k if total[a] is None else total[a] + k
                    total[c] = -k if total[c] is None else total[c] - k
            for a in range(M):
                g = wp[rows] * (smooth(vals[a] - tp[rows]) - total[a] * (1.0 / M))
                gsend[h, a, rows, :] = g.astype(BF)
        for k in range(HM):
            g_copy(h, far + k, 0).start()
        for k in range(1, HM):
            g_copy(h, same_half(k), 1).start()
        gf[h, me] = gsend[h, me]
        for b in range(K // LANES):
            rel, at = b * LANES // B, b * LANES % B
            cols = pl.ds(pl.multiple_of(h * K + LANES * b, LANES), LANES)
            lat_t[:, cols] = lat[rel * PH + h].reshape(B, D)[at : at + LANES, :].T
            hid_t[:, cols] = hid[pl.ds(pl.multiple_of((rel * PH + h) * B + at, LANES), LANES), :].T
        return carry

    with jax.named_scope("pairs"):
        lax.fori_loop(0, PH, phase, 0)

    def back(h, rel):
        blk = 2 * h + rel
        for k in range(HM):
            p = gf[h, (near if rel else far) + k]
            at = pl.multiple_of(blk * B + k * CH, CH)
            gfu[pl.ds(at, PR), :] = p
            gfu[pl.ds(pl.multiple_of(at + PR, CH - PR), CH - PR), :] = unpack_last(p.astype(F32), FD).astype(BF)
        rows = pl.ds(pl.multiple_of(blk * B, B), B)
        held = pl.ds(pl.multiple_of((rel * PH + h) * B, B), B)
        gp[rows, :] = (mm(gfu[rows, :], wh[...]) * slope[held, :]).astype(BF)

    def gather(h):
        arrived(gf.at[h, pl.ds(0, HM - 1)], sem_gr.at[1, h])
        back(h, 1)
        arrived(gf.at[h, pl.ds(0, HM)], sem_gr.at[0, h])
        back(h, 0)

    def terms(h0, phases, i):
        rows = pl.ds(pl.multiple_of(block_of(i) * (2 * r * CN), 2 * r * CN), 2 * r * CN)
        at = slice(h0 * K, (h0 + phases) * K)
        return jnp.concatenate([mm(lat_t[rows, at], gp[at, :]), mm(hid_t[rows, at], gfu[at, :])], axis=1)

    early = [PH - 1, 1]

    with jax.named_scope("early"):
        for h in range(PH - 1):
            gather(h)
            for i, phases in enumerate(early):
                if h < phases:
                    if h == 0:
                        acc[i] = terms(h, 1, i)
                    else:
                        acc[i] += terms(h, 1, i)

    with jax.named_scope("gather"):
        gather(PH - 1)

    def first(i, v):
        for s in range(2):
            for g in range(G):
                at = (s * CN + 2 * g) * r
                low, high = v[at : at + r], v[at + r : at + 2 * r]
                sb[i, s, g] = jnp.where(core == 0, high, low).astype(BF)
                kf[i, s, g] = jnp.where(core == 0, low, high)
        c1(i).start()

    def start_second(i, q):
        for d in range(1, G):
            c2a(i, q, d).start()
        c2b(i, q).start()

    def second(i):
        c1(i).wait_recv()
        for s in range(2):
            for g in range(G):
                v = kf[i, s, g] + r1[i, s, g].astype(F32)
                kf[i, s, g] = v
                s2[i, s, g] = v.astype(BF)

    pieces = [(i, q) for i in range(PB) for q in range(len(chunks))]

    with jax.named_scope("opening"):
        for i in range(PB + 1):
            if i < PB:
                known = early[i] if i < len(early) else 0
                v = terms(known, PH - known, i)
                first(i, v + acc[i] if known else v)
            if i >= 1:
                second(i - 1)
                for j, q in pieces[:AHEAD]:
                    if j == i - 1:
                        start_second(j, q)

    def third(i, q):
        a0, a1, b1 = chunks[q]
        for d in range(1, G):
            c2a(i, q, d).wait_recv()
        away = kf[i, 1 - x, grp, :, a0:a1]
        keep = kf[i, x, grp, :, a0:a1]
        for d in range(1, G):
            away = away + r2a[i, d - 1, 1 - x, :, a0:a1].astype(F32)
            keep = keep + r2a[i, d - 1, x, :, a0:a1].astype(F32)
        s3a[i, :, a0:a1] = away.astype(BF)
        c3a(i, q).start()
        k3[i, :, a0:a1] = keep
        c2b(i, q).wait_recv()
        for g in range(G):
            s3b[i, g, :, a1:b1] = (kf[i, x, g, :, a1:b1] + r2b[i, g, :, a1:b1].astype(F32)).astype(BF)
        for d in range(1, G):
            c3b(i, q, d).start()
        k3[i, :, a1:b1] = kf[i, x, grp, :, a1:b1] + r2b[i, grp, :, a1:b1].astype(F32)

    def fourth(i, q):
        a0, a1, b1 = chunks[q]
        c3a(i, q).wait_recv()
        u = k3[i, :, a0:a1] + r3a[i, :, a0:a1].astype(F32)
        v = k3[i, :, a1:b1]
        for d in range(1, G):
            c3b(i, q, d).wait_recv()
            v = v + r3b[i, d - 1, :, a1:b1].astype(F32)

        if i < PB - 1:
            sz[i, :, a0:a1] = u.astype(BF)
            sz[i, :, a1:b1] = v.astype(BF)
            c4(i, q).start()
        else:
            k3[i, :, a0:a1] = u
            k3[i, :, a1:b1] = v

    with jax.named_scope("stages"):
        for u in range(len(pieces) + BEHIND):
            if u < len(pieces):
                third(*pieces[u])
                if u + AHEAD < len(pieces):
                    start_second(*pieces[u + AHEAD])
            if u >= BEHIND:
                fourth(*pieces[u - BEHIND])

    with jax.named_scope("last"):
        total = k3[PB - 1]
        arrived(rz.at[pl.ds(0, PB - 1)], sem4r.at[0])
        for i in range(PB - 1):
            total = total + rz[i].astype(F32)
        out_in[...] = total[:, :H]
        out_out[...] = total[:, H : H + FD]

    arrived(fsend.at[:, pl.ds(0, M - 1)], sem_fs.at[0])
    arrived(gsend.at[:, pl.ds(0, M - 1)], sem_gs.at[0])
    arrived(sb, sem1s.at[0])
    wide = pl.ds(0, sum(c[1] - c[0] for c in chunks))
    narrow = pl.ds(0, sum(c[2] - c[1] for c in chunks))
    arrived(s2.at[:, :, pl.ds(0, G - 1), :, wide], sem2as.at[0])
    arrived(s2.at[:, 0, :, :, narrow], sem2bs.at[0])
    arrived(s3a.at[:, :, wide], sem3as.at[0])
    arrived(s3b.at[:, pl.ds(0, G - 1), :, narrow], sem3bs.at[0])
    arrived(sz.at[pl.ds(0, PB - 1)], sem4s.at[0])


def publish(res_in, res_out, out_in, out_out, sem):
    a = pltpu.make_async_copy(res_in, out_in, sem.at[0])
    b = pltpu.make_async_copy(res_out, out_out, sem.at[1])
    a.start()
    b.start()
    a.wait()
    b.wait()


def per_device(latent, w_in, w_out, target, cell_mask):
    M = lax.axis_size("member")
    CN = lax.axis_size("cell")
    N, D = latent.shape[1:]
    H = w_in.shape[1]
    FD = w_out.shape[1]
    PH = PHASES
    C = N // M
    CH = C // PH
    K = M * CH
    PB, G = M // 2, CN // 2
    n = FD // (LANES - FD)
    PR = CH // (n + 1) * n
    r = D // (M * CN)
    W = H + LANES
    T = W // LANES
    chunks, at = [], 0
    for tiles in ((T + 1) // 2, T // 2):
        chunks.append((at * LANES, (at + (tiles + 1) // 2) * LANES, (at + tiles) * LANES))
        at += tiles
    NQ = len(chunks)
    NB = -(-(LANES - math.gcd(C, LANES) + C) // LANES)
    GS = max(G - 1, 1)
    V = pltpu.VMEM
    DMA = pltpu.SemaphoreType.DMA
    vm = pl.BlockSpec(memory_space=pltpu.VMEM)
    res = pl.pallas_call(
        functools.partial(body, M, CN, tuple(chunks)),
        out_shape=(V((r, H), F32), V((r, FD), F32)),
        in_specs=[pl.BlockSpec(memory_space=pl.ANY)] * 5,
        out_specs=(vm, vm),
        scratch_shapes=[
            V((2 * PH, M // 2, CH, D), BF), V((D, H), BF), V((LANES, H), BF), V((LANES, H), BF),
            V((FD, N), BF), V((N,), jnp.int32),
            V((N, H), F32), V((N, H), BF), V((N, H), BF), V((N, LANES), BF), V((D, N), BF), V((H, N), BF),
            V((NB * LANES, LANES), F32), V((N, 8), F32),
            V((PH, M, PR, LANES), BF), V((PH, M, PR, LANES), BF), V((PH, M, PR, LANES), BF), V((PH, M, PR, LANES), BF),
            V((2, 2 * CN * r, W), F32), V((PB, 2, G, r, W), F32), V((PB, 2, G, r, W), BF), V((PB, 2, G, r, W), BF),
            V((PB, 2, G, r, W), BF), V((PB, GS, 2, r, W), BF), V((PB, G, r, W), BF),
            V((PB, r, W), F32), V((PB, r, W), BF), V((PB, r, W), BF), V((PB, G, r, W), BF), V((PB, GS, r, W), BF),
            V((PB, r, W), BF), V((PB, r, W), BF),
            DMA((2 * PH + 4,)), DMA((1,)), DMA((PH,)), DMA((1,)), DMA((2, PH)),
            DMA((1,)), DMA((PB,)), DMA((1,)), DMA((NQ, PB, GS)), DMA((1,)), DMA((NQ, PB)),
            DMA((1,)), DMA((NQ, PB)), DMA((1,)), DMA((NQ, PB, GS)), DMA((1,)), DMA((1,)),
        ],
        compiler_params=pltpu.CompilerParams(
            collective_id=0, has_side_effects=True, vmem_limit_bytes=60 * 1024 * 1024
        ),
    )(latent.reshape(M, C, D), w_in, w_out.T, target, cell_mask)
    return pl.pallas_call(
        publish,
        out_shape=(jax.ShapeDtypeStruct((r, H), F32), jax.ShapeDtypeStruct((r, FD), F32)),
        in_specs=[vm, vm],
        out_specs=(pl.BlockSpec(memory_space=pl.ANY),) * 2,
        scratch_shapes=[DMA((2,))],
        compiler_params=pltpu.CompilerParams(vmem_limit_bytes=1024 * 1024),
    )(*(pltpu.with_memory_space_constraint(o, pltpu.VMEM) for o in res))


def solution(mesh):
    in_specs = (P("member", "cell", None), P(), P(), P(None, "cell"), P("cell"))
    out_specs = (P(("member", "cell"), None), P(("member", "cell"), None))
    return jax.shard_map(
        per_device, mesh=mesh, in_specs=in_specs, out_specs=out_specs, check_vma=False
    )
```

```python
import functools
import math

import jax
import jax.numpy as jnp
from jax import lax
from jax.experimental import pallas as pl
from jax.experimental.pallas import tpu as pltpu
from jax.sharding import PartitionSpec as P

MESH = pl.DeviceIdType.MESH
BF = jnp.bfloat16
F32 = jnp.float32
LANES = 128
PHASES = 3
AHEAD = 4
BEHIND = 3
LATE = 1
DIRECT = (1, 3, 0)


def smooth(d):
    return d * lax.rsqrt(1.0 + d * d)


def mm(a, b):
    return jnp.dot(a, b, preferred_element_type=F32)


def pack(f, width):
    spare = LANES - width
    n = width // spare
    q = f.shape[0] // (n + 1)
    lane = lax.broadcasted_iota(jnp.int32, (q, LANES), 1)
    last = f[n * q :]
    parts = []
    for k in range(n):
        parts.append(jnp.where(lane < width, f[k * q : (k + 1) * q], pltpu.roll(last, width - spare * k, 1)))
    return jnp.concatenate(parts, axis=0)


def unpack_last(p, width):
    spare = LANES - width
    n = width // spare
    q = p.shape[0] // n
    lane = lax.broadcasted_iota(jnp.int32, (q, LANES), 1)
    out = pltpu.roll(p[:q], spare, 1)
    for k in range(1, n):
        out = jnp.where(lane < spare * k, out, pltpu.roll(p[k * q : (k + 1) * q], spare * (k + 1), 1))
    return out


def body(
    M, CN, kinds, chunks,
    lat_hbm, w_in_hbm, w_out_hbm, target_hbm, mask_hbm, out_in, out_out,
    lat, w_in, wo, wh, target, mask, slope, hid, gp, gfu, lat_t, hid_t, tgt_t, wgt_t,
    fsend, frecv, gsend, gf,
    acc, kf, sb, r1, s2, r2a, r2b, k3, s3a, r3a, s3b, r3b, sz, rz, r5,
    sem_in, sem_fs, sem_fr, sem_gs, sem_gr,
    sem1s, sem1r, sem2as, sem2ar, sem2bs, sem2br, sem3as, sem3ar, sem3bs, sem3br, sem4s, sem4r, sem5s, sem5r,
):
    me = lax.axis_index("member")
    cell = lax.axis_index("cell")
    core = lax.rem(cell, 2)
    grp = cell // 2
    G = CN // 2
    HM = M // 2
    PB = M // 2
    z = me // 2
    x = lax.rem(me, 2)
    half = me // HM
    near, far = half * HM, (1 - half) * HM
    PH = fsend.shape[0]
    CH, D = lat.shape[2:]
    H = w_in.shape[1]
    FD = w_out_hbm.shape[0]
    B = HM * CH
    K = M * CH
    C = PH * CH
    N = PH * K
    PR = fsend.shape[2]
    W = acc.shape[2]
    r = D // (M * CN)
    scale = 1.0 / (float(N * CN) ** 0.5) / M
    pair_core = (me, grp * 2 + 1 - core)
    pair_x = (me + 1 - 2 * x, cell)

    barrier = pltpu.get_barrier_semaphore()
    for d in range(1, M):
        pl.semaphore_signal(barrier, inc=1, device_id=(lax.rem(me + d, M), cell), device_id_type=MESH)
    pl.semaphore_signal(barrier, inc=1, device_id=pair_core, device_id_type=MESH)
    for d in range(1, G):
        pl.semaphore_signal(
            barrier, inc=1, device_id=(me, lax.rem(grp + d, G) * 2 + core), device_id_type=MESH
        )

    def load(rel, h):
        return pltpu.make_async_copy(
            lat_hbm.at[pl.ds(near if rel else far, HM), pl.ds(h * CH, CH), :],
            lat.at[rel * PH + h],
            sem_in.at[rel * PH + h],
        )

    load_w = pltpu.make_async_copy(w_in_hbm, w_in, sem_in.at[2 * PH])
    load_o = pltpu.make_async_copy(w_out_hbm, wo.at[pl.ds(0, FD), :], sem_in.at[2 * PH + 1])
    load_t = pltpu.make_async_copy(target_hbm, target, sem_in.at[2 * PH + 2])
    load_m = pltpu.make_async_copy(mask_hbm, mask, sem_in.at[2 * PH + 3])
    load_t.start()
    load_m.start()
    load_w.start()
    load(0, 0).start()
    load_o.start()
    for i in range(1, 2 * PH):
        load(i % 2, i // 2).start()
    wo[FD:, :] = jnp.zeros((LANES - FD, H), BF)

    def f_copy(h, t):
        return pltpu.make_async_remote_copy(
            fsend.at[h, t], frecv.at[h, me], sem_fs.at[0], sem_fr.at[h],
            device_id=(t, cell), device_id_type=MESH,
        )

    def g_copy(h, t, rel):
        return pltpu.make_async_remote_copy(
            gsend.at[h, t], gf.at[h, me], sem_gs.at[0], sem_gr.at[rel, h],
            device_id=(t, cell), device_id_type=MESH,
        )

    def arrived(ref, sem):
        pltpu.make_async_copy(ref, ref, sem).wait()

    def same_half(k):
        return near + lax.rem(me + k, HM)

    def c1(i):
        return pltpu.make_async_remote_copy(
            sb.at[i], r1.at[i], sem1s.at[0], sem1r.at[i], device_id=pair_core, device_id_type=MESH
        )

    def c2a(i, q, d):
        cols = pl.ds(chunks[kinds[i]][q][0], chunks[kinds[i]][q][1] - chunks[kinds[i]][q][0])
        g = lax.rem(grp + d, G)
        return pltpu.make_async_remote_copy(
            s2.at[i, :, g, :, cols], r2a.at[i, d - 1, :, :, cols], sem2as.at[kinds[i]], sem2ar.at[q, i, d - 1],
            device_id=(me, g * 2 + core), device_id_type=MESH,
        )

    def c2b(i, q):
        cols = pl.ds(chunks[kinds[i]][q][1], chunks[kinds[i]][q][2] - chunks[kinds[i]][q][1])
        return pltpu.make_async_remote_copy(
            s2.at[i, 1 - x, :, :, cols], r2b.at[i, :, :, cols], sem2bs.at[kinds[i]], sem2br.at[q, i],
            device_id=pair_x, device_id_type=MESH,
        )

    def c3a(i, q):
        cols = pl.ds(chunks[kinds[i]][q][0], chunks[kinds[i]][q][1] - chunks[kinds[i]][q][0])
        return pltpu.make_async_remote_copy(
            s3a.at[i, :, cols], r3a.at[i, :, cols], sem3as.at[kinds[i]], sem3ar.at[q, i],
            device_id=pair_x, device_id_type=MESH,
        )

    def c3b(i, q, d):
        cols = pl.ds(chunks[kinds[i]][q][1], chunks[kinds[i]][q][2] - chunks[kinds[i]][q][1])
        g = lax.rem(grp + d, G)
        return pltpu.make_async_remote_copy(
            s3b.at[i, g, :, cols], r3b.at[i, d - 1, :, cols], sem3bs.at[kinds[i]], sem3br.at[q, i, d - 1],
            device_id=(me, g * 2 + core), device_id_type=MESH,
        )

    HP = PB // 2
    zh = z // HP

    def block_of(i):
        side = (1 - zh) if i < HP else zh
        return side * HP + lax.rem(z + i + 1, HP)

    def c4(i, q):
        cols = pl.ds(chunks[kinds[i]][q][0], chunks[kinds[i]][q][2] - chunks[kinds[i]][q][0])
        return pltpu.make_async_remote_copy(
            sz.at[i, :, cols], rz.at[i, :, cols], sem4s.at[kinds[i]], sem4r.at[kinds[i]],
            device_id=(block_of(i) * 2 + x, cell), device_id_type=MESH,
        )

    def c5(i):
        at = chunks[kinds[i]][-1][2]
        cols = pl.ds(at, W - at)
        return pltpu.make_async_remote_copy(
            s2.at[i, :, :, :, cols], r5.at[i, :, :, :, cols], sem5s.at[i], sem5r.at[i],
            device_id=(block_of(i) * 2 + x, cell), device_id_type=MESH,
        )

    def decode(rel, h):
        at = rel * PH + h
        rows = slice(at * B, (at + 1) * B)
        load(rel, h).wait()
        v = mm(lat[at].reshape(B, D), w_in[...])
        u = 0.5 * v
        t = jnp.tanh(u)
        ut = u * t
        hb = (u + ut).astype(BF)
        slope[rows, :] = (1.0 + t) + (u - ut * t)
        hid[rows, :] = hb
        return lax.dot_general(hb, wo[...], (((1,), (1,)), ((), ())), preferred_element_type=F32)

    def send_fields(rel, h, f):
        for k in range(HM):
            t = (near if rel else far) + k
            fsend[h, t] = pack(f[k * CH : (k + 1) * CH], FD).astype(BF)
            if not rel:
                f_copy(h, t).start()
        if rel:
            frecv[h, me] = fsend[h, me]
            for k in range(1, HM):
                f_copy(h, same_half(k)).start()

    with jax.named_scope("prep"):
        load_t.wait()
        load_m.wait()
        NB = tgt_t.shape[0] // LANES
        b0 = jnp.minimum(me * C // LANES, N // LANES - NB)
        for b in range(NB):
            cols = pl.ds(pl.multiple_of((b0 + b) * LANES, LANES), LANES)
            tgt_t[b * LANES : (b + 1) * LANES, :FD] = target[:, cols].astype(F32).T
        for b in range(N // LANES):
            cols = slice(LANES * b, LANES * b + LANES)
            w = mask[cols].astype(F32) * scale
            wgt_t[cols, :] = jnp.broadcast_to(w[None, :], (8, LANES)).T

    with jax.named_scope("forward"):
        load_w.wait()
        load_o.wait()
        f = decode(0, 0)
        pl.semaphore_wait(barrier, M - 1 + 1 + G - 1)
        send_fields(0, 0, f)
        for i in range(1, 2 * PH):
            send_fields(i % 2, i // 2, decode(i % 2, i // 2))
        wh[...] = (0.5 * wo[...].astype(F32)).astype(BF)

    RB = 16 if PR % 16 == 0 else PR

    def phase(h, carry):
        arrived(frecv.at[h, pl.ds(0, M - 1)], sem_fr.at[h])
        own = pl.multiple_of(me * C - b0 * LANES + h * CH, 8)
        tp = pack(tgt_t[pl.ds(own, CH), :], FD)
        wp = pack(
            jnp.broadcast_to(wgt_t[pl.ds(pl.multiple_of(me * C + h * CH, 8), CH), 0:1], (CH, LANES)), FD
        )
        for b in range(PR // RB):
            rows = slice(b * RB, (b + 1) * RB)
            vals = [frecv[h, j, rows, :].astype(F32) for j in range(M)]
            total = [None] * M
            for a in range(M):
                for c in range(a + 1, M):
                    k = smooth(vals[a] - vals[c])
                    total[a] = k if total[a] is None else total[a] + k
                    total[c] = -k if total[c] is None else total[c] - k
            for a in range(M):
                g = wp[rows] * (smooth(vals[a] - tp[rows]) - total[a] * (1.0 / M))
                gsend[h, a, rows, :] = g.astype(BF)
        for k in range(HM):
            g_copy(h, far + k, 0).start()
        for k in range(1, HM):
            g_copy(h, same_half(k), 1).start()
        gf[h, me] = gsend[h, me]
        for b in range(K // LANES):
            rel, at = b * LANES // B, b * LANES % B
            cols = pl.ds(pl.multiple_of(h * K + LANES * b, LANES), LANES)
            lat_t[:, cols] = lat[rel * PH + h].reshape(B, D)[at : at + LANES, :].T
            hid_t[:, cols] = hid[pl.ds(pl.multiple_of((rel * PH + h) * B + at, LANES), LANES), :].T
        return carry

    with jax.named_scope("pairs"):
        lax.fori_loop(0, PH, phase, 0)

    def back(h, rel):
        blk = 2 * h + rel
        for k in range(HM):
            p = gf[h, (near if rel else far) + k]
            at = pl.multiple_of(blk * B + k * CH, CH)
            gfu[pl.ds(at, PR), :] = p
            gfu[pl.ds(pl.multiple_of(at + PR, CH - PR), CH - PR), :] = unpack_last(p.astype(F32), FD).astype(BF)
        rows = pl.ds(pl.multiple_of(blk * B, B), B)
        held = pl.ds(pl.multiple_of((rel * PH + h) * B, B), B)
        gp[rows, :] = (mm(gfu[rows, :], wh[...]) * slope[held, :]).astype(BF)

    def gather(h):
        arrived(gf.at[h, pl.ds(0, HM - 1)], sem_gr.at[1, h])
        back(h, 1)
        arrived(gf.at[h, pl.ds(0, HM)], sem_gr.at[0, h])
        back(h, 0)

    def terms(h0, phases, i):
        rows = pl.ds(pl.multiple_of(block_of(i) * (2 * r * CN), 2 * r * CN), 2 * r * CN)
        at = slice(h0 * K, (h0 + phases) * K)
        return jnp.concatenate([mm(lat_t[rows, at], gp[at, :]), mm(hid_t[rows, at], gfu[at, :])], axis=1)

    early = [PH - 1, 1]

    with jax.named_scope("early"):
        for h in range(PH - 1):
            gather(h)
            for i, phases in enumerate(early):
                if h < phases:
                    if h == 0:
                        acc[i] = terms(h, 1, i)
                    else:
                        acc[i] += terms(h, 1, i)

    with jax.named_scope("gather"):
        gather(PH - 1)

    def first(i, v):
        for s in range(2):
            for g in range(G):
                at = (s * CN + 2 * g) * r
                low, high = v[at : at + r], v[at + r : at + 2 * r]
                sb[i, s, g] = jnp.where(core == 0, high, low).astype(BF)
                kf[i, s, g] = jnp.where(core == 0, low, high)
        c1(i).start()

    def start_second(i, q):
        for d in range(1, G):
            c2a(i, q, d).start()
        c2b(i, q).start()

    def second(i):
        c1(i).wait_recv()
        for s in range(2):
            for g in range(G):
                v = kf[i, s, g] + r1[i, s, g].astype(F32)
                kf[i, s, g] = v
                s2[i, s, g] = v.astype(BF)
        if i < PB - 1:
            c5(i).start()

    pieces = [(i, q) for i in range(PB) for q in range(2)]

    with jax.named_scope("opening"):
        for i in range(PB + 1):
            if i < PB:
                known = early[i] if i < len(early) else 0
                v = terms(known, PH - known, i)
                first(i, v + acc[i] if known else v)
            if 1 <= i < PB:
                second(i - 1)
                for j, q in pieces[:AHEAD]:
                    if j == i - 1:
                        start_second(j, q)

    def merge():
        for i in range(PB - 1):
            at = chunks[kinds[i]][-1][2]
            c5(i).wait_recv()
            kf[PB - 1, :, :, :, at:] += r5[i, :, :, :, at:].astype(F32)
        at = min(chunks[k][-1][2] for k in kinds)
        s2[PB - 1, :, :, :, at:] = kf[PB - 1, :, :, :, at:].astype(BF)

    def third(i, q):
        a0, a1, b1 = chunks[kinds[i]][q]
        for d in range(1, G):
            c2a(i, q, d).wait_recv()
        away = kf[i, 1 - x, grp, :, a0:a1]
        keep = kf[i, x, grp, :, a0:a1]
        for d in range(1, G):
            away = away + r2a[i, d - 1, 1 - x, :, a0:a1].astype(F32)
            keep = keep + r2a[i, d - 1, x, :, a0:a1].astype(F32)
        s3a[i, :, a0:a1] = away.astype(BF)
        c3a(i, q).start()
        k3[i, :, a0:a1] = keep
        c2b(i, q).wait_recv()
        for g in range(G):
            s3b[i, g, :, a1:b1] = (kf[i, x, g, :, a1:b1] + r2b[i, g, :, a1:b1].astype(F32)).astype(BF)
        for d in range(1, G):
            c3b(i, q, d).start()
        k3[i, :, a1:b1] = kf[i, x, grp, :, a1:b1] + r2b[i, grp, :, a1:b1].astype(F32)

    def fourth(i, q):
        a0, a1, b1 = chunks[kinds[i]][q]
        c3a(i, q).wait_recv()
        u = k3[i, :, a0:a1] + r3a[i, :, a0:a1].astype(F32)
        v = k3[i, :, a1:b1]
        for d in range(1, G):
            c3b(i, q, d).wait_recv()
            v = v + r3b[i, d - 1, :, a1:b1].astype(F32)

        if i < PB - 1:
            sz[i, :, a0:a1] = u.astype(BF)
            sz[i, :, a1:b1] = v.astype(BF)
            c4(i, q).start()
        else:
            k3[i, :, a0:a1] = u
            k3[i, :, a1:b1] = v

    with jax.named_scope("stages"):
        for u in range(len(pieces) + BEHIND):
            if u < len(pieces):
                third(*pieces[u])
                if u == LATE:
                    second(PB - 1)
                if pieces[min(u + AHEAD, len(pieces) - 1)] == (PB - 1, 1) and u + AHEAD < len(pieces):
                    merge()
                if u + AHEAD < len(pieces):
                    start_second(*pieces[u + AHEAD])
            if u >= BEHIND:
                fourth(*pieces[u - BEHIND])

    with jax.named_scope("last"):
        for k in range(2):
            mine = [i for i in range(PB - 1) if kinds[i] == k]
            if mine:
                cols = slice(0, chunks[k][-1][2])
                arrived(rz.at[pl.ds(mine[0], len(mine)), :, cols], sem4r.at[k])
                part = k3[PB - 1, :, cols]
                for i in mine:
                    part = part + rz[i, :, cols].astype(F32)
                k3[PB - 1, :, cols] = part
        total = k3[PB - 1]
        out_in[...] = total[:, :H]
        out_out[...] = total[:, H : H + FD]

    arrived(fsend.at[:, pl.ds(0, M - 1)], sem_fs.at[0])
    arrived(gsend.at[:, pl.ds(0, M - 1)], sem_gs.at[0])
    arrived(sb, sem1s.at[0])
    for k in range(3):
        mine = [i for i in range(PB) if kinds[i] == k]
        if mine:
            at = pl.ds(mine[0], len(mine))
            wide = pl.ds(0, sum(c[1] - c[0] for c in chunks[k]))
            narrow = pl.ds(0, sum(c[2] - c[1] for c in chunks[k]))
            arrived(s2.at[at, :, pl.ds(0, G - 1), :, wide], sem2as.at[k])
            arrived(s2.at[at, 0, :, :, narrow], sem2bs.at[k])
            arrived(s3a.at[at, :, wide], sem3as.at[k])
            arrived(s3b.at[at, pl.ds(0, G - 1), :, narrow], sem3bs.at[k])
            if k < 2:
                arrived(sz.at[at, :, pl.ds(0, chunks[k][-1][2])], sem4s.at[k])
    for i in range(PB - 1):
        c5(i).wait_send()


def publish(res_in, res_out, out_in, out_out, sem):
    a = pltpu.make_async_copy(res_in, out_in, sem.at[0])
    b = pltpu.make_async_copy(res_out, out_out, sem.at[1])
    a.start()
    b.start()
    a.wait()
    b.wait()


def per_device(latent, w_in, w_out, target, cell_mask):
    M = lax.axis_size("member")
    CN = lax.axis_size("cell")
    N, D = latent.shape[1:]
    H = w_in.shape[1]
    FD = w_out.shape[1]
    PH = PHASES
    C = N // M
    CH = C // PH
    K = M * CH
    PB, G = M // 2, CN // 2
    n = FD // (LANES - FD)
    PR = CH // (n + 1) * n
    r = D // (M * CN)
    W = H + LANES
    T = W // LANES
    chunks = []
    for direct in DIRECT:
        tiles, at, cuts = T - direct, 0, []
        for n, a in (((tiles + 1) // 2, 1), (tiles // 2, tiles % 2)):
            cuts.append((at * LANES, (at + (n + a) // 2) * LANES, (at + n) * LANES))
            at += n
        chunks.append(tuple(cuts))
    kinds = tuple(0 if i < PB // 2 else 1 if i < PB - 1 else 2 for i in range(PB))
    NQ = 2
    NB = -(-(LANES - math.gcd(C, LANES) + C) // LANES)
    GS = max(G - 1, 1)
    V = pltpu.VMEM
    DMA = pltpu.SemaphoreType.DMA
    vm = pl.BlockSpec(memory_space=pltpu.VMEM)
    res = pl.pallas_call(
        functools.partial(body, M, CN, kinds, tuple(chunks)),
        out_shape=(V((r, H), F32), V((r, FD), F32)),
        in_specs=[pl.BlockSpec(memory_space=pl.ANY)] * 5,
        out_specs=(vm, vm),
        scratch_shapes=[
            V((2 * PH, M // 2, CH, D), BF), V((D, H), BF), V((LANES, H), BF), V((LANES, H), BF),
            V((FD, N), BF), V((N,), jnp.int32),
            V((N, H), F32), V((N, H), BF), V((N, H), BF), V((N, LANES), BF), V((D, N), BF), V((H, N), BF),
            V((NB * LANES, LANES), F32), V((N, 8), F32),
            V((PH, M, PR, LANES), BF), V((PH, M, PR, LANES), BF), V((PH, M, PR, LANES), BF), V((PH, M, PR, LANES), BF),
            V((2, 2 * CN * r, W), F32), V((PB, 2, G, r, W), F32), V((PB, 2, G, r, W), BF), V((PB, 2, G, r, W), BF),
            V((PB, 2, G, r, W), BF), V((PB, GS, 2, r, W), BF), V((PB, G, r, W), BF),
            V((PB, r, W), F32), V((PB, r, W), BF), V((PB, r, W), BF), V((PB, G, r, W), BF), V((PB, GS, r, W), BF),
            V((PB, r, W), BF), V((PB, r, W), BF), V((PB - 1, 2, G, r, W), BF),
            DMA((2 * PH + 4,)), DMA((1,)), DMA((PH,)), DMA((1,)), DMA((2, PH)),
            DMA((1,)), DMA((PB,)), DMA((3,)), DMA((NQ, PB, GS)), DMA((3,)), DMA((NQ, PB)),
            DMA((3,)), DMA((NQ, PB)), DMA((3,)), DMA((NQ, PB, GS)), DMA((2,)), DMA((2,)), DMA((PB - 1,)), DMA((PB - 1,)),
        ],
        compiler_params=pltpu.CompilerParams(
            collective_id=0, has_side_effects=True, vmem_limit_bytes=60 * 1024 * 1024
        ),
    )(latent.reshape(M, C, D), w_in, w_out.T, target, cell_mask)
    return pl.pallas_call(
        publish,
        out_shape=(jax.ShapeDtypeStruct((r, H), F32), jax.ShapeDtypeStruct((r, FD), F32)),
        in_specs=[vm, vm],
        out_specs=(pl.BlockSpec(memory_space=pl.ANY),) * 2,
        scratch_shapes=[DMA((2,))],
        compiler_params=pltpu.CompilerParams(vmem_limit_bytes=1024 * 1024),
    )(*(pltpu.with_memory_space_constraint(o, pltpu.VMEM) for o in res))


def solution(mesh):
    in_specs = (P("member", "cell", None), P(), P(), P(None, "cell"), P("cell"))
    out_specs = (P(("member", "cell"), None), P(("member", "cell"), None))
    return jax.shard_map(
        per_device, mesh=mesh, in_specs=in_specs, out_specs=out_specs, check_vma=False
    )
```

```python
import functools
import math

import jax
import jax.numpy as jnp
from jax import lax
from jax.experimental import pallas as pl
from jax.experimental.pallas import tpu as pltpu
from jax.sharding import PartitionSpec as P

MESH = pl.DeviceIdType.MESH
BF = jnp.bfloat16
F32 = jnp.float32
LANES = 128
PHASES = 3
AHEAD = 4
BEHIND = 3
LATE = 1
JOIN = 4
DIRECT = (1,3,0)


def smooth(d):
    return d * lax.rsqrt(1.0 + d * d)


def mm(a, b):
    return jnp.dot(a, b, preferred_element_type=F32)


def pack(f, width):
    spare = LANES - width
    n = width // spare
    q = f.shape[0] // (n + 1)
    lane = lax.broadcasted_iota(jnp.int32, (q, LANES), 1)
    last = f[n * q :]
    parts = []
    for k in range(n):
        parts.append(jnp.where(lane < width, f[k * q : (k + 1) * q], pltpu.roll(last, width - spare * k, 1)))
    return jnp.concatenate(parts, axis=0)


def unpack_last(p, width):
    spare = LANES - width
    n = width // spare
    q = p.shape[0] // n
    lane = lax.broadcasted_iota(jnp.int32, (q, LANES), 1)
    out = pltpu.roll(p[:q], spare, 1)
    for k in range(1, n):
        out = jnp.where(lane < spare * k, out, pltpu.roll(p[k * q : (k + 1) * q], spare * (k + 1), 1))
    return out


def body(
    M, CN, kinds, chunks,
    lat_hbm, w_in_hbm, w_out_hbm, target_hbm, mask_hbm, out_in, out_out,
    lat, w_in, wo, wh, target, mask, slope, hid, gp, gfu, lat_t, hid_t, tgt_t, wgt_t,
    fsend, frecv, gsend, gf,
    acc, kf, sb, r1, s2, r2a, r2b, k3, s3a, r3a, s3b, r3b, sz, rz, r5,
    sem_in, sem_fs, sem_fr, sem_gs, sem_gr,
    sem1s, sem1r, sem2as, sem2ar, sem2bs, sem2br, sem3as, sem3ar, sem3bs, sem3br, sem4s, sem4r, sem5s, sem5r,
):
    me = lax.axis_index("member")
    cell = lax.axis_index("cell")
    core = lax.rem(cell, 2)
    grp = cell // 2
    G = CN // 2
    HM = M // 2
    PB = M // 2
    z = me // 2
    x = lax.rem(me, 2)
    half = me // HM
    near, far = half * HM, (1 - half) * HM
    PH = fsend.shape[0]
    CH, D = lat.shape[2:]
    H = w_in.shape[1]
    FD = w_out_hbm.shape[0]
    B = HM * CH
    K = M * CH
    C = PH * CH
    N = PH * K
    PR = fsend.shape[2]
    W = acc.shape[2]
    r = D // (M * CN)
    scale = 1.0 / (float(N * CN) ** 0.5) / M
    pair_core = (me, grp * 2 + 1 - core)
    pair_x = (me + 1 - 2 * x, cell)

    barrier = pltpu.get_barrier_semaphore()
    for d in range(1, M):
        pl.semaphore_signal(barrier, inc=1, device_id=(lax.rem(me + d, M), cell), device_id_type=MESH)
    pl.semaphore_signal(barrier, inc=1, device_id=pair_core, device_id_type=MESH)
    for d in range(1, G):
        pl.semaphore_signal(
            barrier, inc=1, device_id=(me, lax.rem(grp + d, G) * 2 + core), device_id_type=MESH
        )

    def load(rel, h):
        return pltpu.make_async_copy(
            lat_hbm.at[pl.ds(near if rel else far, HM), pl.ds(h * CH, CH), :],
            lat.at[rel * PH + h],
            sem_in.at[rel * PH + h],
        )

    load_w = pltpu.make_async_copy(w_in_hbm, w_in, sem_in.at[2 * PH])
    load_o = pltpu.make_async_copy(w_out_hbm, wo.at[pl.ds(0, FD), :], sem_in.at[2 * PH + 1])
    load_t = pltpu.make_async_copy(target_hbm, target, sem_in.at[2 * PH + 2])
    load_m = pltpu.make_async_copy(mask_hbm, mask, sem_in.at[2 * PH + 3])
    load_t.start()
    load_m.start()
    load_w.start()
    load(0, 0).start()
    load_o.start()
    for i in range(1, 2 * PH):
        load(i % 2, i // 2).start()
    wo[FD:, :] = jnp.zeros((LANES - FD, H), BF)

    def f_copy(h, t):
        return pltpu.make_async_remote_copy(
            fsend.at[h, t], frecv.at[h, me], sem_fs.at[0], sem_fr.at[h],
            device_id=(t, cell), device_id_type=MESH,
        )

    def g_copy(h, t, rel):
        return pltpu.make_async_remote_copy(
            gsend.at[h, t], gf.at[h, me], sem_gs.at[0], sem_gr.at[rel, h],
            device_id=(t, cell), device_id_type=MESH,
        )

    def arrived(ref, sem):
        pltpu.make_async_copy(ref, ref, sem).wait()

    def same_half(k):
        return near + lax.rem(me + k, HM)

    def c1(i):
        return pltpu.make_async_remote_copy(
            sb.at[i], r1.at[i], sem1s.at[0], sem1r.at[i], device_id=pair_core, device_id_type=MESH
        )

    def c2a(i, q, d):
        cols = pl.ds(chunks[kinds[i]][q][0], chunks[kinds[i]][q][1] - chunks[kinds[i]][q][0])
        g = lax.rem(grp + d, G)
        return pltpu.make_async_remote_copy(
            s2.at[i, :, g, :, cols], r2a.at[i, d - 1, :, :, cols], sem2as.at[kinds[i]], sem2ar.at[q, i, d - 1],
            device_id=(me, g * 2 + core), device_id_type=MESH,
        )

    def c2b(i, q):
        cols = pl.ds(chunks[kinds[i]][q][1], chunks[kinds[i]][q][2] - chunks[kinds[i]][q][1])
        return pltpu.make_async_remote_copy(
            s2.at[i, 1 - x, :, :, cols], r2b.at[i, :, :, cols], sem2bs.at[kinds[i]], sem2br.at[q, i],
            device_id=pair_x, device_id_type=MESH,
        )

    def c3a(i, q):
        cols = pl.ds(chunks[kinds[i]][q][0], chunks[kinds[i]][q][1] - chunks[kinds[i]][q][0])
        return pltpu.make_async_remote_copy(
            s3a.at[i, :, cols], r3a.at[i, :, cols], sem3as.at[kinds[i]], sem3ar.at[q, i],
            device_id=pair_x, device_id_type=MESH,
        )

    def c3b(i, q, d):
        cols = pl.ds(chunks[kinds[i]][q][1], chunks[kinds[i]][q][2] - chunks[kinds[i]][q][1])
        g = lax.rem(grp + d, G)
        return pltpu.make_async_remote_copy(
            s3b.at[i, g, :, cols], r3b.at[i, d - 1, :, cols], sem3bs.at[kinds[i]], sem3br.at[q, i, d - 1],
            device_id=(me, g * 2 + core), device_id_type=MESH,
        )

    HP = PB // 2
    zh = z // HP

    def block_of(i):
        side = (1 - zh) if i < HP else zh
        return side * HP + lax.rem(z + i + 1, HP)

    def c4(i, q):
        cols = pl.ds(chunks[kinds[i]][q][0], chunks[kinds[i]][q][2] - chunks[kinds[i]][q][0])
        return pltpu.make_async_remote_copy(
            sz.at[i, :, cols], rz.at[i, :, cols], sem4s.at[kinds[i]], sem4r.at[kinds[i]],
            device_id=(block_of(i) * 2 + x, cell), device_id_type=MESH,
        )

    def c5(i):
        at = chunks[kinds[i]][-1][2]
        cols = pl.ds(at, W - at)
        return pltpu.make_async_remote_copy(
            s2.at[i, :, :, :, cols], r5.at[i, :, :, :, cols], sem5s.at[i], sem5r.at[i],
            device_id=(block_of(i) * 2 + x, cell), device_id_type=MESH,
        )

    def decode(rel, h):
        at = rel * PH + h
        rows = slice(at * B, (at + 1) * B)
        load(rel, h).wait()
        v = mm(lat[at].reshape(B, D), w_in[...])
        u = 0.5 * v
        t = jnp.tanh(u)
        ut = u * t
        hb = (u + ut).astype(BF)
        slope[rows, :] = (1.0 + t) + (u - ut * t)
        hid[rows, :] = hb
        return lax.dot_general(hb, wo[...], (((1,), (1,)), ((), ())), preferred_element_type=F32)

    def send_fields(rel, h, f):
        for k in range(HM):
            t = (near if rel else far) + k
            fsend[h, t] = pack(f[k * CH : (k + 1) * CH], FD).astype(BF)
            if not rel:
                f_copy(h, t).start()
        if rel:
            frecv[h, me] = fsend[h, me]
            for k in range(1, HM):
                f_copy(h, same_half(k)).start()

    with jax.named_scope("prep"):
        load_t.wait()
        load_m.wait()
        NB = tgt_t.shape[0] // LANES
        b0 = jnp.minimum(me * C // LANES, N // LANES - NB)
        for b in range(NB):
            cols = pl.ds(pl.multiple_of((b0 + b) * LANES, LANES), LANES)
            tgt_t[b * LANES : (b + 1) * LANES, :FD] = target[:, cols].astype(F32).T
        for b in range(N // LANES):
            cols = slice(LANES * b, LANES * b + LANES)
            w = mask[cols].astype(F32) * scale
            wgt_t[cols, :] = jnp.broadcast_to(w[None, :], (8, LANES)).T

    with jax.named_scope("forward"):
        load_w.wait()
        load_o.wait()
        f = decode(0, 0)
        pl.semaphore_wait(barrier, M - 1 + 1 + G - 1)
        send_fields(0, 0, f)
        for i in range(1, 2 * PH):
            send_fields(i % 2, i // 2, decode(i % 2, i // 2))
        wh[...] = (0.5 * wo[...].astype(F32)).astype(BF)

    RB = 16 if PR % 16 == 0 else PR

    def phase(h, carry):
        arrived(frecv.at[h, pl.ds(0, M - 1)], sem_fr.at[h])
        own = pl.multiple_of(me * C - b0 * LANES + h * CH, 8)
        tp = pack(tgt_t[pl.ds(own, CH), :], FD)
        wp = pack(
            jnp.broadcast_to(wgt_t[pl.ds(pl.multiple_of(me * C + h * CH, 8), CH), 0:1], (CH, LANES)), FD
        )
        for b in range(PR // RB):
            rows = slice(b * RB, (b + 1) * RB)
            vals = [frecv[h, j, rows, :].astype(F32) for j in range(M)]
            total = [None] * M
            for a in range(M):
                for c in range(a + 1, M):
                    k = smooth(vals[a] - vals[c])
                    total[a] = k if total[a] is None else total[a] + k
                    total[c] = -k if total[c] is None else total[c] - k
            for a in range(M):
                g = wp[rows] * (smooth(vals[a] - tp[rows]) - total[a] * (1.0 / M))
                gsend[h, a, rows, :] = g.astype(BF)
        for k in range(HM):
            g_copy(h, far + k, 0).start()
        for k in range(1, HM):
            g_copy(h, same_half(k), 1).start()
        gf[h, me] = gsend[h, me]
        for b in range(K // LANES):
            rel, at = b * LANES // B, b * LANES % B
            cols = pl.ds(pl.multiple_of(h * K + LANES * b, LANES), LANES)
            lat_t[:, cols] = lat[rel * PH + h].reshape(B, D)[at : at + LANES, :].T
            hid_t[:, cols] = hid[pl.ds(pl.multiple_of((rel * PH + h) * B + at, LANES), LANES), :].T
        return carry

    with jax.named_scope("pairs"):
        lax.fori_loop(0, PH, phase, 0)

    def back(h, rel):
        blk = 2 * h + rel
        for k in range(HM):
            p = gf[h, (near if rel else far) + k]
            at = pl.multiple_of(blk * B + k * CH, CH)
            gfu[pl.ds(at, PR), :] = p
            gfu[pl.ds(pl.multiple_of(at + PR, CH - PR), CH - PR), :] = unpack_last(p.astype(F32), FD).astype(BF)
        rows = pl.ds(pl.multiple_of(blk * B, B), B)
        held = pl.ds(pl.multiple_of((rel * PH + h) * B, B), B)
        gp[rows, :] = (mm(gfu[rows, :], wh[...]) * slope[held, :]).astype(BF)

    def gather(h):
        arrived(gf.at[h, pl.ds(0, HM - 1)], sem_gr.at[1, h])
        back(h, 1)
        arrived(gf.at[h, pl.ds(0, HM)], sem_gr.at[0, h])
        back(h, 0)

    def terms(h0, phases, i):
        rows = pl.ds(pl.multiple_of(block_of(i) * (2 * r * CN), 2 * r * CN), 2 * r * CN)
        at = slice(h0 * K, (h0 + phases) * K)
        return jnp.concatenate([mm(lat_t[rows, at], gp[at, :]), mm(hid_t[rows, at], gfu[at, :])], axis=1)

    early = [PH - 1, 1]

    with jax.named_scope("early"):
        for h in range(PH - 1):
            gather(h)
            for i, phases in enumerate(early):
                if h < phases:
                    if h == 0:
                        acc[i] = terms(h, 1, i)
                    else:
                        acc[i] += terms(h, 1, i)

    with jax.named_scope("gather"):
        gather(PH - 1)

    def first(i, v):
        for s in range(2):
            for g in range(G):
                at = (s * CN + 2 * g) * r
                low, high = v[at : at + r], v[at + r : at + 2 * r]
                sb[i, s, g] = jnp.where(core == 0, high, low).astype(BF)
                kf[i, s, g] = jnp.where(core == 0, low, high)
        c1(i).start()

    def start_second(i, q):
        for d in range(1, G):
            c2a(i, q, d).start()
        c2b(i, q).start()

    def second(i):
        c1(i).wait_recv()
        for s in range(2):
            for g in range(G):
                v = kf[i, s, g] + r1[i, s, g].astype(F32)
                kf[i, s, g] = v
                s2[i, s, g] = v.astype(BF)
        if i < PB - 1:
            c5(i).start()

    pieces = [(i, q) for i in range(PB) for q in range(2)]

    with jax.named_scope("opening"):
        for i in range(PB + 1):
            if i < PB:
                known = early[i] if i < len(early) else 0
                v = terms(known, PH - known, i)
                first(i, v + acc[i] if known else v)
            if 1 <= i < PB:
                second(i - 1)
                for j, q in pieces[:AHEAD]:
                    if j == i - 1:
                        start_second(j, q)

    def merge():
        for i in range(PB - 1):
            at = chunks[kinds[i]][-1][2]
            c5(i).wait_recv()
            kf[PB - 1, :, :, :, at:] += r5[i, :, :, :, at:].astype(F32)
        at = min(chunks[k][-1][2] for k in kinds)
        s2[PB - 1, :, :, :, at:] = kf[PB - 1, :, :, :, at:].astype(BF)

    def third(i, q):
        a0, a1, b1 = chunks[kinds[i]][q]
        for d in range(1, G):
            c2a(i, q, d).wait_recv()
        away = kf[i, 1 - x, grp, :, a0:a1]
        keep = kf[i, x, grp, :, a0:a1]
        for d in range(1, G):
            away = away + r2a[i, d - 1, 1 - x, :, a0:a1].astype(F32)
            keep = keep + r2a[i, d - 1, x, :, a0:a1].astype(F32)
        s3a[i, :, a0:a1] = away.astype(BF)
        c3a(i, q).start()
        k3[i, :, a0:a1] = keep
        c2b(i, q).wait_recv()
        for g in range(G):
            s3b[i, g, :, a1:b1] = (kf[i, x, g, :, a1:b1] + r2b[i, g, :, a1:b1].astype(F32)).astype(BF)
        for d in range(1, G):
            c3b(i, q, d).start()
        k3[i, :, a1:b1] = kf[i, x, grp, :, a1:b1] + r2b[i, grp, :, a1:b1].astype(F32)

    def fourth(i, q):
        a0, a1, b1 = chunks[kinds[i]][q]
        c3a(i, q).wait_recv()
        u = k3[i, :, a0:a1] + r3a[i, :, a0:a1].astype(F32)
        v = k3[i, :, a1:b1]
        for d in range(1, G):
            c3b(i, q, d).wait_recv()
            v = v + r3b[i, d - 1, :, a1:b1].astype(F32)

        if i < PB - 1:
            sz[i, :, a0:a1] = u.astype(BF)
            sz[i, :, a1:b1] = v.astype(BF)
            c4(i, q).start()
        else:
            k3[i, :, a0:a1] = u
            k3[i, :, a1:b1] = v

    with jax.named_scope("stages"):
        for u in range(len(pieces) + BEHIND):
            if u < len(pieces):
                third(*pieces[u])
                if u == LATE:
                    second(PB - 1)
                if u + AHEAD < len(pieces) - 1:
                    start_second(*pieces[u + AHEAD])
            if u >= BEHIND:
                fourth(*pieces[u - BEHIND])
            if u == len(pieces) - JOIN:
                merge()
                start_second(*pieces[-1])

    with jax.named_scope("last"):
        for k in range(2):
            mine = [i for i in range(PB - 1) if kinds[i] == k]
            if mine:
                cols = slice(0, chunks[k][-1][2])
                arrived(rz.at[pl.ds(mine[0], len(mine)), :, cols], sem4r.at[k])
                part = k3[PB - 1, :, cols]
                for i in mine:
                    part = part + rz[i, :, cols].astype(F32)
                k3[PB - 1, :, cols] = part
        total = k3[PB - 1]
        out_in[...] = total[:, :H]
        out_out[...] = total[:, H : H + FD]

    arrived(fsend.at[:, pl.ds(0, M - 1)], sem_fs.at[0])
    arrived(gsend.at[:, pl.ds(0, M - 1)], sem_gs.at[0])
    arrived(sb, sem1s.at[0])
    for k in range(3):
        mine = [i for i in range(PB) if kinds[i] == k]
        if mine:
            at = pl.ds(mine[0], len(mine))
            wide = pl.ds(0, sum(c[1] - c[0] for c in chunks[k]))
            narrow = pl.ds(0, sum(c[2] - c[1] for c in chunks[k]))
            arrived(s2.at[at, :, pl.ds(0, G - 1), :, wide], sem2as.at[k])
            arrived(s2.at[at, 0, :, :, narrow], sem2bs.at[k])
            arrived(s3a.at[at, :, wide], sem3as.at[k])
            arrived(s3b.at[at, pl.ds(0, G - 1), :, narrow], sem3bs.at[k])
            if k < 2:
                arrived(sz.at[at, :, pl.ds(0, chunks[k][-1][2])], sem4s.at[k])
    for i in range(PB - 1):
        c5(i).wait_send()


def publish(res_in, res_out, out_in, out_out, sem):
    a = pltpu.make_async_copy(res_in, out_in, sem.at[0])
    b = pltpu.make_async_copy(res_out, out_out, sem.at[1])
    a.start()
    b.start()
    a.wait()
    b.wait()


def per_device(latent, w_in, w_out, target, cell_mask):
    M = lax.axis_size("member")
    CN = lax.axis_size("cell")
    N, D = latent.shape[1:]
    H = w_in.shape[1]
    FD = w_out.shape[1]
    PH = PHASES
    C = N // M
    CH = C // PH
    K = M * CH
    PB, G = M // 2, CN // 2
    n = FD // (LANES - FD)
    PR = CH // (n + 1) * n
    r = D // (M * CN)
    W = H + LANES
    T = W // LANES
    chunks = []
    for direct in DIRECT:
        tiles, at, cuts = T - direct, 0, []
        for n, a in (((tiles + 1) // 2, 1), (tiles // 2, tiles % 2)):
            cuts.append((at * LANES, (at + (n + a) // 2) * LANES, (at + n) * LANES))
            at += n
        chunks.append(tuple(cuts))
    kinds = tuple(0 if i < PB // 2 else 1 if i < PB - 1 else 2 for i in range(PB))
    NQ = 2
    NB = -(-(LANES - math.gcd(C, LANES) + C) // LANES)
    GS = max(G - 1, 1)
    V = pltpu.VMEM
    DMA = pltpu.SemaphoreType.DMA
    vm = pl.BlockSpec(memory_space=pltpu.VMEM)
    res = pl.pallas_call(
        functools.partial(body, M, CN, kinds, tuple(chunks)),
        out_shape=(V((r, H), F32), V((r, FD), F32)),
        in_specs=[pl.BlockSpec(memory_space=pl.ANY)] * 5,
        out_specs=(vm, vm),
        scratch_shapes=[
            V((2 * PH, M // 2, CH, D), BF), V((D, H), BF), V((LANES, H), BF), V((LANES, H), BF),
            V((FD, N), BF), V((N,), jnp.int32),
            V((N, H), F32), V((N, H), BF), V((N, H), BF), V((N, LANES), BF), V((D, N), BF), V((H, N), BF),
            V((NB * LANES, LANES), F32), V((N, 8), F32),
            V((PH, M, PR, LANES), BF), V((PH, M, PR, LANES), BF), V((PH, M, PR, LANES), BF), V((PH, M, PR, LANES), BF),
            V((2, 2 * CN * r, W), F32), V((PB, 2, G, r, W), F32), V((PB, 2, G, r, W), BF), V((PB, 2, G, r, W), BF),
            V((PB, 2, G, r, W), BF), V((PB, GS, 2, r, W), BF), V((PB, G, r, W), BF),
            V((PB, r, W), F32), V((PB, r, W), BF), V((PB, r, W), BF), V((PB, G, r, W), BF), V((PB, GS, r, W), BF),
            V((PB, r, W), BF), V((PB, r, W), BF), V((PB - 1, 2, G, r, W), BF),
            DMA((2 * PH + 4,)), DMA((1,)), DMA((PH,)), DMA((1,)), DMA((2, PH)),
            DMA((1,)), DMA((PB,)), DMA((3,)), DMA((NQ, PB, GS)), DMA((3,)), DMA((NQ, PB)),
            DMA((3,)), DMA((NQ, PB)), DMA((3,)), DMA((NQ, PB, GS)), DMA((2,)), DMA((2,)), DMA((PB - 1,)), DMA((PB - 1,)),
        ],
        compiler_params=pltpu.CompilerParams(
            collective_id=0, has_side_effects=True, vmem_limit_bytes=60 * 1024 * 1024
        ),
    )(latent.reshape(M, C, D), w_in, w_out.T, target, cell_mask)
    return pl.pallas_call(
        publish,
        out_shape=(jax.ShapeDtypeStruct((r, H), F32), jax.ShapeDtypeStruct((r, FD), F32)),
        in_specs=[vm, vm],
        out_specs=(pl.BlockSpec(memory_space=pl.ANY),) * 2,
        scratch_shapes=[DMA((2,))],
        compiler_params=pltpu.CompilerParams(vmem_limit_bytes=1024 * 1024),
    )(*(pltpu.with_memory_space_constraint(o, pltpu.VMEM) for o in res))


def solution(mesh):
    in_specs = (P("member", "cell", None), P(), P(), P(None, "cell"), P("cell"))
    out_specs = (P(("member", "cell"), None), P(("member", "cell"), None))
    return jax.shard_map(
        per_device, mesh=mesh, in_specs=in_specs, out_specs=out_specs, check_vma=False
    )
```

```python
import functools
import math

import jax
import jax.numpy as jnp
from jax import lax
from jax.experimental import pallas as pl
from jax.experimental.pallas import tpu as pltpu
from jax.sharding import PartitionSpec as P

MESH = pl.DeviceIdType.MESH
BF = jnp.bfloat16
F32 = jnp.float32
LANES = 128
PHASES = 3
AHEAD = 4
BEHIND = 3
LATE = 1
JOIN = 4
DIRECT = (1,3,0)


def smooth(d):
    return d * lax.rsqrt(1.0 + d * d)


def mm(a, b):
    return jnp.dot(a, b, preferred_element_type=F32)


def pack(f, width):
    spare = LANES - width
    n = width // spare
    q = f.shape[0] // (n + 1)
    lane = lax.broadcasted_iota(jnp.int32, (q, LANES), 1)
    last = f[n * q :]
    parts = []
    for k in range(n):
        parts.append(jnp.where(lane < width, f[k * q : (k + 1) * q], pltpu.roll(last, width - spare * k, 1)))
    return jnp.concatenate(parts, axis=0)


def unpack_last(p, width):
    spare = LANES - width
    n = width // spare
    q = p.shape[0] // n
    lane = lax.broadcasted_iota(jnp.int32, (q, LANES), 1)
    out = pltpu.roll(p[:q], spare, 1)
    for k in range(1, n):
        out = jnp.where(lane < spare * k, out, pltpu.roll(p[k * q : (k + 1) * q], spare * (k + 1), 1))
    return out


def body(
    M, CN, kinds, chunks,
    lat_hbm, w_in_hbm, w_out_hbm, target_hbm, mask_hbm, out_in, out_out,
    lat, w_in, wo, wh, target, mask, slope, hid, gp, gfu, lat_t, hid_t, tgt_t, wgt_t,
    fsend, frecv, gsend, gf,
    acc, kf, sb, r1, s2, r2a, r2b, k3, s3a, r3a, s3b, r3b, sz, rz, r5,
    sem_in, sem_fs, sem_fr, sem_gs, sem_gr,
    sem1s, sem1r, sem2as, sem2ar, sem2bs, sem2br, sem3as, sem3ar, sem3bs, sem3br, sem4s, sem4r, sem5s, sem5r,
):
    me = lax.axis_index("member")
    cell = lax.axis_index("cell")
    core = lax.rem(cell, 2)
    grp = cell // 2
    G = CN // 2
    HM = M // 2
    PB = M // 2
    z = me // 2
    x = lax.rem(me, 2)
    half = me // HM
    near, far = half * HM, (1 - half) * HM
    PH = fsend.shape[0]
    CH, D = lat.shape[2:]
    H = w_in.shape[1]
    FD = w_out_hbm.shape[0]
    B = HM * CH
    K = M * CH
    C = PH * CH
    N = PH * K
    PR = fsend.shape[2]
    W = acc.shape[2]
    r = D // (M * CN)
    scale = 1.0 / (float(N * CN) ** 0.5) / M
    pair_core = (me, grp * 2 + 1 - core)
    pair_x = (me + 1 - 2 * x, cell)

    barrier = pltpu.get_barrier_semaphore()
    for d in range(1, M):
        pl.semaphore_signal(barrier, inc=1, device_id=(lax.rem(me + d, M), cell), device_id_type=MESH)
    pl.semaphore_signal(barrier, inc=1, device_id=pair_core, device_id_type=MESH)
    for d in range(1, G):
        pl.semaphore_signal(
            barrier, inc=1, device_id=(me, lax.rem(grp + d, G) * 2 + core), device_id_type=MESH
        )

    def load(rel, h):
        return pltpu.make_async_copy(
            lat_hbm.at[pl.ds(near if rel else far, HM), pl.ds(h * CH, CH), :],
            lat.at[rel * PH + h],
            sem_in.at[rel * PH + h],
        )

    load_w = pltpu.make_async_copy(w_in_hbm, w_in, sem_in.at[2 * PH])
    load_o = pltpu.make_async_copy(w_out_hbm, wo.at[pl.ds(0, FD), :], sem_in.at[2 * PH + 1])
    load_t = pltpu.make_async_copy(target_hbm, target, sem_in.at[2 * PH + 2])
    load_m = pltpu.make_async_copy(mask_hbm, mask, sem_in.at[2 * PH + 3])
    load_t.start()
    load_m.start()
    load_w.start()
    load(0, 0).start()
    load_o.start()
    for i in range(1, 2 * PH):
        load(i % 2, i // 2).start()
    wo[FD:, :] = jnp.zeros((LANES - FD, H), BF)

    def f_copy(h, t):
        return pltpu.make_async_remote_copy(
            fsend.at[h, t], frecv.at[h, me], sem_fs.at[0], sem_fr.at[h],
            device_id=(t, cell), device_id_type=MESH,
        )

    def g_copy(h, t, rel):
        return pltpu.make_async_remote_copy(
            gsend.at[h, t], gf.at[h, me], sem_gs.at[0], sem_gr.at[rel, h],
            device_id=(t, cell), device_id_type=MESH,
        )

    def arrived(ref, sem):
        pltpu.make_async_copy(ref, ref, sem).wait()

    def same_half(k):
        return near + lax.rem(me + k, HM)

    def c1(i):
        return pltpu.make_async_remote_copy(
            sb.at[i], r1.at[i], sem1s.at[0], sem1r.at[i], device_id=pair_core, device_id_type=MESH
        )

    def c2a(i, q, d):
        cols = pl.ds(chunks[kinds[i]][q][0], chunks[kinds[i]][q][1] - chunks[kinds[i]][q][0])
        g = lax.rem(grp + d, G)
        return pltpu.make_async_remote_copy(
            s2.at[i, :, g, :, cols], r2a.at[i, d - 1, :, :, cols], sem2as.at[kinds[i]], sem2ar.at[q, i, d - 1],
            device_id=(me, g * 2 + core), device_id_type=MESH,
        )

    def c2b(i, q):
        cols = pl.ds(chunks[kinds[i]][q][1], chunks[kinds[i]][q][2] - chunks[kinds[i]][q][1])
        return pltpu.make_async_remote_copy(
            s2.at[i, 1 - x, :, :, cols], r2b.at[i, :, :, cols], sem2bs.at[kinds[i]], sem2br.at[q, i],
            device_id=pair_x, device_id_type=MESH,
        )

    def c3a(i, q):
        cols = pl.ds(chunks[kinds[i]][q][0], chunks[kinds[i]][q][1] - chunks[kinds[i]][q][0])
        return pltpu.make_async_remote_copy(
            s3a.at[i, :, cols], r3a.at[i, :, cols], sem3as.at[kinds[i]], sem3ar.at[q, i],
            device_id=pair_x, device_id_type=MESH,
        )

    def c3b(i, q, d):
        cols = pl.ds(chunks[kinds[i]][q][1], chunks[kinds[i]][q][2] - chunks[kinds[i]][q][1])
        g = lax.rem(grp + d, G)
        return pltpu.make_async_remote_copy(
            s3b.at[i, g, :, cols], r3b.at[i, d - 1, :, cols], sem3bs.at[kinds[i]], sem3br.at[q, i, d - 1],
            device_id=(me, g * 2 + core), device_id_type=MESH,
        )

    HP = PB // 2
    zh = z // HP

    def block_of(i):
        side = (1 - zh) if i < HP else zh
        return side * HP + lax.rem(z + i + 1, HP)

    def c4(i, q):
        cols = pl.ds(chunks[kinds[i]][q][0], chunks[kinds[i]][q][2] - chunks[kinds[i]][q][0])
        return pltpu.make_async_remote_copy(
            sz.at[i, :, cols], rz.at[i, :, cols], sem4s.at[kinds[i]], sem4r.at[kinds[i]],
            device_id=(block_of(i) * 2 + x, cell), device_id_type=MESH,
        )

    def c5(i):
        at = chunks[kinds[i]][-1][2]
        cols = pl.ds(at, W - at)
        return pltpu.make_async_remote_copy(
            s2.at[i, :, :, :, cols], r5.at[i, :, :, :, cols], sem5s.at[i], sem5r.at[i],
            device_id=(block_of(i) * 2 + x, cell), device_id_type=MESH,
        )

    def decode(rel, h):
        at = rel * PH + h
        rows = slice(at * B, (at + 1) * B)
        load(rel, h).wait()
        v = mm(lat[at].reshape(B, D), w_in[...])
        u = 0.5 * v
        t = jnp.tanh(u)
        ut = u * t
        hb = (u + ut).astype(BF)
        slope[rows, :] = (1.0 + t) + (u - ut * t)
        hid[rows, :] = hb
        return lax.dot_general(hb, wo[...], (((1,), (1,)), ((), ())), preferred_element_type=F32)

    def send_fields(rel, h, f):
        for k in range(HM):
            t = (near if rel else far) + k
            fsend[h, t] = pack(f[k * CH : (k + 1) * CH], FD).astype(BF)
            if not rel:
                f_copy(h, t).start()
        if rel:
            frecv[h, me] = fsend[h, me]
            for k in range(1, HM):
                f_copy(h, same_half(k)).start()

    with jax.named_scope("prep"):
        load_t.wait()
        load_m.wait()
        NB = tgt_t.shape[0] // LANES
        b0 = jnp.minimum(me * C // LANES, N // LANES - NB)
        for b in range(NB):
            cols = pl.ds(pl.multiple_of((b0 + b) * LANES, LANES), LANES)
            tgt_t[b * LANES : (b + 1) * LANES, :FD] = target[:, cols].astype(F32).T
        for b in range(N // LANES):
            cols = slice(LANES * b, LANES * b + LANES)
            w = mask[cols].astype(F32) * scale
            wgt_t[cols, :] = jnp.broadcast_to(w[None, :], (8, LANES)).T

    with jax.named_scope("forward"):
        load_w.wait()
        load_o.wait()
        f = decode(0, 0)
        pl.semaphore_wait(barrier, M - 1 + 1 + G - 1)
        send_fields(0, 0, f)
        for i in range(1, 2 * PH):
            send_fields(i % 2, i // 2, decode(i % 2, i // 2))
        wh[...] = (0.5 * wo[...].astype(F32)).astype(BF)

    RB = 16 if PR % 16 == 0 else PR

    def phase(h, carry):
        arrived(frecv.at[h, pl.ds(0, M - 1)], sem_fr.at[h])
        own = pl.multiple_of(me * C - b0 * LANES + h * CH, 8)
        tp = pack(tgt_t[pl.ds(own, CH), :], FD)
        wp = pack(
            jnp.broadcast_to(wgt_t[pl.ds(pl.multiple_of(me * C + h * CH, 8), CH), 0:1], (CH, LANES)), FD
        )
        for b in range(PR // RB):
            rows = slice(b * RB, (b + 1) * RB)
            vals = [frecv[h, j, rows, :].astype(F32) for j in range(M)]
            total = [None] * M
            for a in range(M):
                for c in range(a + 1, M):
                    k = smooth(vals[a] - vals[c])
                    total[a] = k if total[a] is None else total[a] + k
                    total[c] = -k if total[c] is None else total[c] - k
            for a in range(M):
                g = wp[rows] * (smooth(vals[a] - tp[rows]) - total[a] * (1.0 / M))
                gsend[h, a, rows, :] = g.astype(BF)
        for k in range(HM):
            g_copy(h, far + k, 0).start()
        for k in range(1, HM):
            g_copy(h, same_half(k), 1).start()
        gf[h, me] = gsend[h, me]
        for b in range(K // LANES):
            rel, at = b * LANES // B, b * LANES % B
            cols = pl.ds(pl.multiple_of(h * K + LANES * b, LANES), LANES)
            lat_t[:, cols] = lat[rel * PH + h].reshape(B, D)[at : at + LANES, :].T
            hid_t[:, cols] = hid[pl.ds(pl.multiple_of((rel * PH + h) * B + at, LANES), LANES), :].T
        return carry

    with jax.named_scope("pairs"):
        lax.fori_loop(0, PH, phase, 0)

    def back(h, rel):
        blk = 2 * h + rel
        for k in range(HM):
            p = gf[h, (near if rel else far) + k]
            at = pl.multiple_of(blk * B + k * CH, CH)
            gfu[pl.ds(at, PR), :] = p
            gfu[pl.ds(pl.multiple_of(at + PR, CH - PR), CH - PR), :] = unpack_last(p.astype(F32), FD).astype(BF)
        rows = pl.ds(pl.multiple_of(blk * B, B), B)
        held = pl.ds(pl.multiple_of((rel * PH + h) * B, B), B)
        gp[rows, :] = (mm(gfu[rows, :], wh[...]) * slope[held, :]).astype(BF)

    def gather(h):
        arrived(gf.at[h, pl.ds(0, HM - 1)], sem_gr.at[1, h])
        back(h, 1)
        arrived(gf.at[h, pl.ds(0, HM)], sem_gr.at[0, h])
        back(h, 0)

    def terms(h0, phases, i):
        rows = pl.ds(pl.multiple_of(block_of(i) * (2 * r * CN), 2 * r * CN), 2 * r * CN)
        at = slice(h0 * K, (h0 + phases) * K)
        return jnp.concatenate([mm(lat_t[rows, at], gp[at, :]), mm(hid_t[rows, at], gfu[at, :])], axis=1)

    early = [PH - 1, 1]

    with jax.named_scope("early"):
        for h in range(PH - 1):
            gather(h)
            for i, phases in enumerate(early):
                if h < phases:
                    if h == 0:
                        acc[i] = terms(h, 1, i)
                    else:
                        acc[i] += terms(h, 1, i)

    with jax.named_scope("gather"):
        gather(PH - 1)

    def first(i, v):
        for s in range(2):
            for g in range(G):
                at = (s * CN + 2 * g) * r
                low, high = v[at : at + r], v[at + r : at + 2 * r]
                sb[i, s, g] = jnp.where(core == 0, high, low).astype(BF)
                kf[i, s, g] = jnp.where(core == 0, low, high)
        c1(i).start()

    def start_second(i, q):
        for d in range(1, G):
            c2a(i, q, d).start()
        c2b(i, q).start()

    def second(i):
        c1(i).wait_recv()
        for s in range(2):
            for g in range(G):
                v = kf[i, s, g] + r1[i, s, g].astype(F32)
                kf[i, s, g] = v
                s2[i, s, g] = v.astype(BF)
        if i < PB - 1:
            c5(i).start()

    pieces = [(i, q) for i in range(PB) for q in range(2)]

    with jax.named_scope("opening"):
        for i in range(PB + 1):
            if i < PB:
                known = early[i] if i < len(early) else 0
                v = terms(known, PH - known, i)
                first(i, v + acc[i] if known else v)
            if 1 <= i < PB:
                second(i - 1)
                for j, q in pieces[:AHEAD]:
                    if j == i - 1:
                        start_second(j, q)

    def merge():
        for i in range(PB - 1):
            at = chunks[kinds[i]][-1][2]
            c5(i).wait_recv()
            kf[PB - 1, :, :, :, at:] += r5[i, :, :, :, at:].astype(F32)
        at = min(chunks[k][-1][2] for k in kinds)
        s2[PB - 1, :, :, :, at:] = kf[PB - 1, :, :, :, at:].astype(BF)

    def third(i, q):
        a0, a1, b1 = chunks[kinds[i]][q]
        for d in range(1, G):
            c2a(i, q, d).wait_recv()
        away = kf[i, 1 - x, grp, :, a0:a1]
        keep = kf[i, x, grp, :, a0:a1]
        for d in range(1, G):
            away = away + r2a[i, d - 1, 1 - x, :, a0:a1].astype(F32)
            keep = keep + r2a[i, d - 1, x, :, a0:a1].astype(F32)
        s3a[i, :, a0:a1] = away.astype(BF)
        c3a(i, q).start()
        k3[i, :, a0:a1] = keep
        c2b(i, q).wait_recv()
        for g in range(G):
            s3b[i, g, :, a1:b1] = (kf[i, x, g, :, a1:b1] + r2b[i, g, :, a1:b1].astype(F32)).astype(BF)
        for d in range(1, G):
            c3b(i, q, d).start()
        k3[i, :, a1:b1] = kf[i, x, grp, :, a1:b1] + r2b[i, grp, :, a1:b1].astype(F32)

    def fourth(i, q):
        a0, a1, b1 = chunks[kinds[i]][q]
        c3a(i, q).wait_recv()
        u = k3[i, :, a0:a1] + r3a[i, :, a0:a1].astype(F32)
        v = k3[i, :, a1:b1]
        for d in range(1, G):
            c3b(i, q, d).wait_recv()
            v = v + r3b[i, d - 1, :, a1:b1].astype(F32)

        if i < PB - 1:
            sz[i, :, a0:a1] = u.astype(BF)
            sz[i, :, a1:b1] = v.astype(BF)
            c4(i, q).start()
        else:
            k3[i, :, a0:a1] = u
            k3[i, :, a1:b1] = v

    with jax.named_scope("stages"):
        for u in range(len(pieces) + BEHIND):
            if u < len(pieces):
                third(*pieces[u])
                if u == LATE:
                    second(PB - 1)
                if u + AHEAD < len(pieces) - 1:
                    start_second(*pieces[u + AHEAD])
            if u >= BEHIND:
                fourth(*pieces[u - BEHIND])
            if u == len(pieces) - JOIN:
                merge()
                start_second(*pieces[-1])

    arrived(fsend.at[:, pl.ds(0, M - 1)], sem_fs.at[0])
    arrived(gsend.at[:, pl.ds(0, M - 1)], sem_gs.at[0])
    arrived(sb, sem1s.at[0])
    for k in range(3):
        mine = [i for i in range(PB) if kinds[i] == k]
        if mine:
            at = pl.ds(mine[0], len(mine))
            wide = pl.ds(0, sum(c[1] - c[0] for c in chunks[k]))
            narrow = pl.ds(0, sum(c[2] - c[1] for c in chunks[k]))
            arrived(s2.at[at, :, pl.ds(0, G - 1), :, wide], sem2as.at[k])
            arrived(s2.at[at, 0, :, :, narrow], sem2bs.at[k])
            arrived(s3a.at[at, :, wide], sem3as.at[k])
            arrived(s3b.at[at, pl.ds(0, G - 1), :, narrow], sem3bs.at[k])
    for i in range(PB - 1):
        c5(i).wait_send()

    with jax.named_scope("last"):
        for k in range(2):
            mine = [i for i in range(PB - 1) if kinds[i] == k]
            if mine:
                cols = slice(0, chunks[k][-1][2])
                arrived(rz.at[pl.ds(mine[0], len(mine)), :, cols], sem4r.at[k])
                part = k3[PB - 1, :, cols]
                for i in mine:
                    part = part + rz[i, :, cols].astype(F32)
                k3[PB - 1, :, cols] = part
        total = k3[PB - 1]
        out_in[...] = total[:, :H]
        out_out[...] = total[:, H : H + FD]

    for k in range(2):
        mine = [i for i in range(PB) if kinds[i] == k]
        if mine:
            arrived(sz.at[pl.ds(mine[0], len(mine)), :, pl.ds(0, chunks[k][-1][2])], sem4s.at[k])


def publish(res_in, res_out, out_in, out_out, sem):
    a = pltpu.make_async_copy(res_in, out_in, sem.at[0])
    b = pltpu.make_async_copy(res_out, out_out, sem.at[1])
    a.start()
    b.start()
    a.wait()
    b.wait()


def per_device(latent, w_in, w_out, target, cell_mask):
    M = lax.axis_size("member")
    CN = lax.axis_size("cell")
    N, D = latent.shape[1:]
    H = w_in.shape[1]
    FD = w_out.shape[1]
    PH = PHASES
    C = N // M
    CH = C // PH
    K = M * CH
    PB, G = M // 2, CN // 2
    n = FD // (LANES - FD)
    PR = CH // (n + 1) * n
    r = D // (M * CN)
    W = H + LANES
    T = W // LANES
    chunks = []
    for direct in DIRECT:
        tiles, at, cuts = T - direct, 0, []
        for n, a in (((tiles + 1) // 2, 1), (tiles // 2, tiles % 2)):
            cuts.append((at * LANES, (at + (n + a) // 2) * LANES, (at + n) * LANES))
            at += n
        chunks.append(tuple(cuts))
    kinds = tuple(0 if i < PB // 2 else 1 if i < PB - 1 else 2 for i in range(PB))
    NQ = 2
    NB = -(-(LANES - math.gcd(C, LANES) + C) // LANES)
    GS = max(G - 1, 1)
    V = pltpu.VMEM
    DMA = pltpu.SemaphoreType.DMA
    vm = pl.BlockSpec(memory_space=pltpu.VMEM)
    res = pl.pallas_call(
        functools.partial(body, M, CN, kinds, tuple(chunks)),
        out_shape=(V((r, H), F32), V((r, FD), F32)),
        in_specs=[pl.BlockSpec(memory_space=pl.ANY)] * 5,
        out_specs=(vm, vm),
        scratch_shapes=[
            V((2 * PH, M // 2, CH, D), BF), V((D, H), BF), V((LANES, H), BF), V((LANES, H), BF),
            V((FD, N), BF), V((N,), jnp.int32),
            V((N, H), F32), V((N, H), BF), V((N, H), BF), V((N, LANES), BF), V((D, N), BF), V((H, N), BF),
            V((NB * LANES, LANES), F32), V((N, 8), F32),
            V((PH, M, PR, LANES), BF), V((PH, M, PR, LANES), BF), V((PH, M, PR, LANES), BF), V((PH, M, PR, LANES), BF),
            V((2, 2 * CN * r, W), F32), V((PB, 2, G, r, W), F32), V((PB, 2, G, r, W), BF), V((PB, 2, G, r, W), BF),
            V((PB, 2, G, r, W), BF), V((PB, GS, 2, r, W), BF), V((PB, G, r, W), BF),
            V((PB, r, W), F32), V((PB, r, W), BF), V((PB, r, W), BF), V((PB, G, r, W), BF), V((PB, GS, r, W), BF),
            V((PB, r, W), BF), V((PB, r, W), BF), V((PB - 1, 2, G, r, W), BF),
            DMA((2 * PH + 4,)), DMA((1,)), DMA((PH,)), DMA((1,)), DMA((2, PH)),
            DMA((1,)), DMA((PB,)), DMA((3,)), DMA((NQ, PB, GS)), DMA((3,)), DMA((NQ, PB)),
            DMA((3,)), DMA((NQ, PB)), DMA((3,)), DMA((NQ, PB, GS)), DMA((2,)), DMA((2,)), DMA((PB - 1,)), DMA((PB - 1,)),
        ],
        compiler_params=pltpu.CompilerParams(
            collective_id=0, has_side_effects=True, vmem_limit_bytes=60 * 1024 * 1024
        ),
    )(latent.reshape(M, C, D), w_in, w_out.T, target, cell_mask)
    return pl.pallas_call(
        publish,
        out_shape=(jax.ShapeDtypeStruct((r, H), F32), jax.ShapeDtypeStruct((r, FD), F32)),
        in_specs=[vm, vm],
        out_specs=(pl.BlockSpec(memory_space=pl.ANY),) * 2,
        scratch_shapes=[DMA((2,))],
        compiler_params=pltpu.CompilerParams(vmem_limit_bytes=1024 * 1024),
    )(*(pltpu.with_memory_space_constraint(o, pltpu.VMEM) for o in res))


def solution(mesh):
    in_specs = (P("member", "cell", None), P(), P(), P(None, "cell"), P("cell"))
    out_specs = (P(("member", "cell"), None), P(("member", "cell"), None))
    return jax.shard_map(
        per_device, mesh=mesh, in_specs=in_specs, out_specs=out_specs, check_vma=False
    )
```
